128 devices in a mesh: section: 4 (over x), vertex: 16 (over z, y), feat: 2 (over core).
Axes of the slice: x: 4, y: 4, z: 4, core: 2. Of those that a mesh axis runs over, the one named last changes fastest.
Arguments:
- features: bfloat16 [32768, 1024], P('vertex', 'feat'), may hold values from -6 to 6
- history: bfloat16 [4, 32768, 1024], P('section', 'vertex', 'feat'), may hold values from -6 to 6
- weights: bfloat16 [4, 1024, 1024], P('section', None, 'feat'), may hold values from -0.1875 to 0.1875
- tile_values: bfloat16 [3, 1024, 128, 128], P(None, 'vertex'), may hold values from -0.125 to 0.125
- tile_rows: int32 [3, 1024], P(None, 'vertex'), may hold values from 0 to 15, as said below
- tile_cols: int32 [3, 1024], P(None, 'vertex'), may hold values from 0 to 15
- tile_counts: int32 [3, 16], P(None, 'vertex'), may hold values from 1 to 64, as said below
- span_ids: int32 [3, 2048], P(None, 'vertex'), may hold values from 0 to 2047, as said below
Outputs:
- layer_out: bfloat16 [4, 3, 2048, 1024], P('section', None, 'vertex', 'feat')
- new_history: bfloat16 [4, 32768, 1024], P('section', 'vertex', 'feat')
The draws below stay inside these ranges and needn't reach their ends.
Inputs may be any that keep to these rules, and one draw needn't show every extreme that they name: `tile_rows`: within one owner's list for one block the (row block, column block) pairs are distinct. `tile_counts`: in every block some owner has exactly 64 live tiles. `span_ids`: the 384 entries of one owner over all blocks are distinct.
All inputs are finite; a program needn't handle non-finite values.
Results may differ from the reference program's by a relative error of at most 0.018.
Values may be sent and summed in bfloat16 or wider, within the bound.
No kernel may reach another device: no remote copies, remote signals or barrier semaphores. Data moves between devices by JAX's collectives and lax.ppermute only.
A program may use at most 128 MiB of HBM per device.

```python
import math
import jax
import jax.numpy as jnp
from jax import lax

F = 1024
BLOCK = 128
SPANS = 3
ROWS_DEV = 128
VD = 2048
LAYERS = 4
V = 32768
TILES = 64
N_SECTION = 4
N_VERTEX = 16


def tile_pairs(key):
    row_blocks = ROWS_DEV * N_VERTEX // BLOCK
    col_blocks = VD // BLOCK
    keys = jax.random.split(jax.random.fold_in(key, 11), SPANS * N_VERTEX)
    picks = jax.vmap(lambda single: jax.random.permutation(single, row_blocks * col_blocks)[:TILES])(keys)
    return (picks.reshape(SPANS, N_VERTEX * TILES).astype(jnp.int32), col_blocks)


def draw_tile_rows(key, part):
    picks, col_blocks = tile_pairs(key)
    return (picks // col_blocks).astype(jnp.int32)


def draw_tile_cols(key, part):
    picks, col_blocks = tile_pairs(key)
    return (picks % col_blocks).astype(jnp.int32)


def draw_tile_counts(key, part):
    lowest = max(1, TILES // 8)
    base = jax.random.randint(jax.random.fold_in(key, 5), (SPANS, N_VERTEX), lowest, TILES // 2 + 1)
    busiest = jax.random.randint(jax.random.fold_in(key, 6), (SPANS, 1), 0, N_VERTEX)
    owner_index = jnp.arange(N_VERTEX)[None, :]
    return jnp.where(owner_index == busiest, TILES, base).astype(jnp.int32)


def draw_span_ids(key, part):
    keys = jax.random.split(jax.random.fold_in(key, 17), N_VERTEX)
    picks = jax.vmap(lambda single: jax.random.permutation(single, VD)[:SPANS * ROWS_DEV])(keys)
    picks = picks.reshape(N_VERTEX, SPANS, ROWS_DEV).transpose(1, 0, 2)
    return picks.reshape(SPANS, N_VERTEX * ROWS_DEV).astype(jnp.int32)


def levels(key, shape, shards, least, top_value):
    factor_of, own = 1.0, jax.random.fold_in(key, 6)
    for position, blocks in shards:
        draws = jnp.exp(jax.random.uniform(jax.random.fold_in(own, position), (blocks,), jnp.float32, least / len(shards), top_value / len(shards)))
        factor_of = factor_of * jnp.repeat(draws, shape[position] // blocks).reshape([-1 if axis == position else 1 for axis in range(len(shape))])
    return factor_of


def bell_draw(rng, shape, width, limit, cuts=(), dtype=jnp.bfloat16):
    values = width * jax.random.normal(rng, shape, jnp.float32)
    if cuts:
        values = values * levels(rng, shape, cuts, -0.22, 0.18)
    return jnp.clip(values, -limit, limit).astype(dtype)


def setup_inputs(seed: int = 0) -> dict:
    splits = jax.random.split(jax.random.key(seed), 9)
    features = bell_draw(splits[0], (V, F), 1.0, 6.0, ((0, 16), (1, 2)))
    history = bell_draw(splits[1], (LAYERS, V, F), 1.0, 6.0, ((0, 4), (1, 16), (2, 2)))
    weights = bell_draw(splits[2], (LAYERS, F, F), F ** -0.5, 0.1875, ((0, 4), (2, 2)))
    tile_values = bell_draw(splits[3], (SPANS, N_VERTEX * TILES, BLOCK, BLOCK), (N_VERTEX * VD // 16) ** -0.5, 0.125, ((1, 16),))
    tile_rows = draw_tile_rows(jax.random.fold_in(splits[8], 71), 0)
    tile_cols = draw_tile_cols(jax.random.fold_in(splits[8], 71), 0)
    tile_counts = draw_tile_counts(jax.random.fold_in(splits[8], 71), 0)
    span_ids = draw_span_ids(jax.random.fold_in(splits[8], 71), 0)
    return {"features": features, "history": history, "weights": weights, "tile_values": tile_values, "tile_rows": tile_rows, "tile_cols": tile_cols, "tile_counts": tile_counts, "span_ids": span_ids}


RESIDUAL_SHARE = 0.2
BETA_SCALE = 0.5


def reference(features, history, weights, tile_values, tile_rows, tile_cols, tile_counts, span_ids):
    row_blocks = ROWS_DEV * N_VERTEX // BLOCK
    col_blocks = VD // BLOCK
    owners = (jnp.arange(ROWS_DEV * N_VERTEX) // ROWS_DEV).astype(jnp.int32) * VD
    outputs = []
    tables = []
    previous = None
    for layer in range(N_SECTION):
        table = history[layer]
        beta_rate = math.log(BETA_SCALE / (layer + 1) + 1.0)
        results = []
        for span_index in range(SPANS):
            vertex_ids = span_ids[span_index].astype(jnp.int32) + owners
            initial = features[vertex_ids]
            fresh_rows = initial if layer == 0 else previous[span_index]
            table = table.at[vertex_ids].set(fresh_rows)
            blocks = table.reshape(N_VERTEX * col_blocks, BLOCK, F)
            values_here = tile_values[span_index]
            rows_here = tile_rows[span_index]
            cols_here = tile_cols[span_index]
            counts_here = tile_counts[span_index]

            def device_term(device, running):
                first = (device * TILES).astype(jnp.int32)
                tile_block = lax.dynamic_slice_in_dim(values_here, first, TILES, 0).astype(jnp.float32)
                row_ids = lax.dynamic_slice_in_dim(rows_here, first, TILES, 0)
                col_ids = lax.dynamic_slice_in_dim(cols_here, first, TILES, 0) + (device * col_blocks).astype(jnp.int32)
                alive = (jnp.arange(TILES) < counts_here[device]).astype(jnp.float32)
                picked = blocks[col_ids].astype(jnp.float32)
                products = jnp.einsum("tij,tjc->tic", tile_block, picked, precision=lax.Precision.HIGHEST)
                products = products * alive[:, None, None]
                summed = jax.ops.segment_sum(products, row_ids, num_segments=row_blocks)
                rounded = lax.optimization_barrier(summed.astype(jnp.bfloat16))
                return running + rounded.astype(jnp.float32)

            aggregate = lax.fori_loop(0, N_VERTEX, device_term, jnp.zeros((row_blocks, BLOCK, F), jnp.float32))
            aggregate = aggregate.reshape(ROWS_DEV * N_VERTEX, F)
            support = ((1.0 - RESIDUAL_SHARE) * aggregate + RESIDUAL_SHARE * initial.astype(jnp.float32)).astype(jnp.bfloat16)
            projected = jnp.dot(support, weights[layer], preferred_element_type=jnp.float32)
            layer_rows = jax.nn.relu((1.0 - beta_rate) * support.astype(jnp.float32) + beta_rate * projected).astype(jnp.bfloat16)
            results.append(layer_rows)
        previous = results
        outputs.append(jnp.stack(results))
        tables.append(table)
    return jnp.stack(outputs), jnp.stack(tables)
```

```python
import math

import jax
import jax.numpy as jnp
from jax import lax
from jax.experimental import pallas as pl
from jax.experimental.pallas import tpu as pltpu
from jax.sharding import PartitionSpec as P

RESIDUAL_SHARE = 0.2
BETA_SCALE = 0.5
MIB = 1 << 20


def rotated(array, axis, by):
    devices = lax.axis_size(axis)
    return lax.ppermute(array, axis, [(i, (i + by) % devices) for i in range(devices)])


def vmem_params(mib):
    return pltpu.CompilerParams(vmem_limit_bytes=mib * MIB)


def dense_adjacency(tile_values, tile_rows, tile_cols, tile_counts, row_blocks, col_blocks):
    spans, slots, side, _ = tile_values.shape
    rows, cols = row_blocks * side, col_blocks * side

    def kernel(rows_ref, cols_ref, counts_ref, values_ref, out_ref):
        span = pl.program_id(0)
        out_ref[...] = jnp.zeros_like(out_ref)

        @pl.loop(0, counts_ref[span])
        def _(slot):
            row = pl.multiple_of(rows_ref[span, slot] * side, side)
            col = pl.multiple_of(cols_ref[span, slot] * side, side)
            out_ref[0, pl.ds(row, side), pl.ds(col, side)] = values_ref[0, slot]

    return pl.pallas_call(
        kernel,
        out_shape=jax.ShapeDtypeStruct((spans, rows, cols), jnp.bfloat16),
        grid_spec=pltpu.PrefetchScalarGridSpec(
            num_scalar_prefetch=3,
            grid=(spans,),
            in_specs=[pl.BlockSpec((1, slots, side, side), lambda c, *_: (c, 0, 0, 0))],
            out_specs=pl.BlockSpec((1, rows, cols), lambda c, *_: (c, 0, 0)),
        ),
        compiler_params=vmem_params(40),
        cost_estimate=pl.CostEstimate(
            flops=0, transcendentals=0, bytes_accessed=2 * spans * (rows * cols + slots * side * side)
        ),
        name="dense_adjacency",
    )(tile_rows, tile_cols, tile_counts[:, 0], tile_values)


def first_partial(adjacency, hist, feats, replaced, row_devices):
    spans, rows, cols = adjacency.shape
    width = hist.shape[1]
    rows_local = rows // row_devices
    step = 2

    def kernel(adj_ref, hist_ref, feat_ref, mask_ref, out_ref, table):
        table[...] = jnp.where(mask_ref[0] > 0, feat_ref[...], hist_ref[...])
        for first in range(0, row_devices, step):
            part = jnp.dot(
                adj_ref[0, first * rows_local : (first + step) * rows_local, :],
                table[...],
                preferred_element_type=jnp.float32,
            )
            out_ref[first : first + step, 0] = part.astype(jnp.bfloat16).reshape(
                step, rows_local, width
            )

    return pl.pallas_call(
        kernel,
        out_shape=jax.ShapeDtypeStruct((row_devices, spans, rows_local, width), jnp.bfloat16),
        grid=(spans,),
        in_specs=[
            pl.BlockSpec((1, rows, cols), lambda c: (c, 0, 0)),
            pl.BlockSpec((cols, width), lambda c: (0, 0)),
            pl.BlockSpec((cols, width), lambda c: (0, 0)),
            pl.BlockSpec((1, cols, width), lambda c: (c, 0, 0)),
        ],
        out_specs=pl.BlockSpec((row_devices, 1, rows_local, width), lambda c: (0, c, 0, 0)),
        scratch_shapes=[pltpu.VMEM((cols, width), jnp.bfloat16)],
        compiler_params=vmem_params(40),
        cost_estimate=pl.CostEstimate(
            flops=2 * spans * rows * cols * width,
            transcendentals=0,
            bytes_accessed=2 * spans * (rows * cols + rows * width),
        ),
        name="first_partial",
    )(adjacency, hist, feats, replaced)


def static_parts(adjacency, hist_slices, replaced, select):
    spans, rows, cols = adjacency.shape
    layers, _, width = hist_slices.shape
    later = layers - 1
    picks = select.shape[1]
    chunk = 256

    def kernel(adj_ref, hist_ref, mask_ref, sel_ref, static_ref, cols_ref, right):
        for layer in range(later):
            right[:, layer * width : (layer + 1) * width] = jnp.where(
                mask_ref[0] > 0, jnp.zeros_like(hist_ref[0]), hist_ref[layer + 1]
            )
        right[:, later * width :] = sel_ref[...]
        for first in range(0, rows, chunk):
            part = jnp.dot(
                adj_ref[0, first : first + chunk, :], right[...], preferred_element_type=jnp.float32
            )
            for layer in range(later):
                static_ref[layer, 0, first : first + chunk] = part[
                    :, layer * width : (layer + 1) * width
                ]
            cols_ref[0, first : first + chunk] = part[:, later * width :].astype(jnp.bfloat16)

    return pl.pallas_call(
        kernel,
        out_shape=(
            jax.ShapeDtypeStruct((later, spans, rows, width), jnp.float32),
            jax.ShapeDtypeStruct((spans, rows, picks), jnp.bfloat16),
        ),
        grid=(spans,),
        in_specs=[
            pl.BlockSpec((1, rows, cols), lambda c: (c, 0, 0)),
            pl.BlockSpec((layers, cols, width), lambda c: (0, 0, 0)),
            pl.BlockSpec((1, cols, width), lambda c: (c, 0, 0)),
            pl.BlockSpec((cols, picks), lambda c: (0, 0)),
        ],
        out_specs=(
            pl.BlockSpec((later, 1, rows, width), lambda c: (0, c, 0, 0)),
            pl.BlockSpec((1, rows, picks), lambda c: (c, 0, 0)),
        ),
        scratch_shapes=[pltpu.VMEM((cols, later * width + picks), jnp.bfloat16)],
        compiler_params=vmem_params(48),
        cost_estimate=pl.CostEstimate(
            flops=2 * spans * rows * cols * (later * width + picks),
            transcendentals=0,
            bytes_accessed=spans * (2 * rows * cols + 4 * later * rows * width + 2 * rows * picks),
        ),
        name="static_parts",
    )(adjacency, hist_slices, replaced, select)


def layer_step(gathered, support, weight_rows, static, columns, beta, row_devices):
    halves, parts, picks, width = gathered.shape
    spans, rows, _ = columns.shape
    rows_local = rows // row_devices
    depth = halves * parts * width
    step = 4

    def kernel(gath_ref, sup_ref, w_ref, static_ref, cols_ref, out_ref, left):
        for half in range(halves):
            for part in range(parts):
                first = (half * parts + part) * width
                left[:, first : first + width] = gath_ref[half, part]
        projected = jnp.dot(left[...], w_ref[...], preferred_element_type=jnp.float32)
        fresh = jnp.maximum(
            (1.0 - beta) * sup_ref[...].astype(jnp.float32) + beta * projected, 0.0
        ).astype(jnp.bfloat16)
        for span in range(spans):
            used = (span + 1) * rows_local
            for first in range(0, row_devices, step):
                at = slice(first * rows_local, (first + step) * rows_local)
                part = static_ref[span, at] + jnp.dot(
                    cols_ref[span, at, :used], fresh[:used], preferred_element_type=jnp.float32
                )
                out_ref[first : first + step, span] = part.astype(jnp.bfloat16).reshape(
                    step, rows_local, width
                )

    return pl.pallas_call(
        kernel,
        out_shape=jax.ShapeDtypeStruct((row_devices, spans, rows_local, width), jnp.bfloat16),
        scratch_shapes=[pltpu.VMEM((picks, depth), jnp.bfloat16)],
        compiler_params=vmem_params(40),
        cost_estimate=pl.CostEstimate(
            flops=2 * picks * depth * width + 4 * rows * width * picks,
            transcendentals=0,
            bytes_accessed=6 * spans * rows * width + 2 * spans * rows * picks,
        ),
        name="layer_step",
    )(gathered, support, weight_rows, static, columns)


def whole_rows(gathered, own_half, weight_cols, beta):
    halves, parts, picks, width = gathered.shape
    full = jnp.transpose(gathered, (2, 0, 1, 3)).reshape(picks, halves * parts * width)
    projected = jnp.dot(full, weight_cols, preferred_element_type=jnp.float32)
    return jax.nn.relu(
        (1.0 - beta) * own_half.astype(jnp.float32) + beta * projected
    ).astype(jnp.bfloat16)


def shards(features, history, weights, tile_values, tile_rows, tile_cols, tile_counts, span_ids):
    spans, rows_local = span_ids.shape
    side = tile_values.shape[2]
    owned, half = features.shape
    layers = lax.axis_size("section")
    halves = lax.axis_size("feat")
    row_devices = lax.axis_size("vertex")
    section = lax.axis_index("section")
    feat = lax.axis_index("feat")
    width = half // layers
    picks = spans * rows_local
    depth = weights.shape[1]
    betas = [math.log(BETA_SCALE / (layer + 1) + 1.0) for layer in range(layers)]

    def column_slices(array):
        return jnp.transpose(array.reshape(array.shape[0], layers, width), (1, 0, 2))

    stored = history[0]
    hist_slices = lax.all_to_all(column_slices(stored), "section", 0, 0, tiled=True)
    weight_slices = lax.all_to_all(column_slices(weights[0]), "section", 0, 0, tiled=True)
    weights_before = rotated(weights[0], "section", 1)

    ids = span_ids.reshape(picks)
    hits = jnp.arange(owned)[:, None] == ids[None, :]
    select = hits.astype(jnp.bfloat16)
    upto = jnp.stack([jnp.any(hits[:, : (c + 1) * rows_local], axis=1) for c in range(spans)])
    replaced = jnp.broadcast_to(upto[:, :, None], (spans, owned, width)).astype(jnp.bfloat16)

    feat_slice = lax.dynamic_slice_in_dim(features, section * width, width, 1)
    initial_half = jnp.take(features, ids, axis=0)
    initial = lax.dynamic_slice_in_dim(initial_half, section * width, width, 1).astype(jnp.float32)

    adjacency = dense_adjacency(
        tile_values, tile_rows, tile_cols, tile_counts, rows_local * row_devices // side, owned // side
    )
    partial = first_partial(adjacency, hist_slices[0], feat_slice, replaced, row_devices)
    statics, columns = static_parts(adjacency, hist_slices, replaced, select)

    order = (section - jnp.arange(layers)) % layers
    def in_order(weight):
        blocks = weight.reshape(halves, layers, width, weight.shape[-1])
        return jnp.take(blocks, order, axis=1).reshape(depth, weight.shape[-1])

    slices_ordered = [in_order(weight_slices[layer]) for layer in range(layers)]
    own_ordered = in_order(weights[0])
    before_ordered = in_order(weights_before)

    kept = kept_before = None
    for layer in range(layers):
        arrived = lax.all_to_all(partial, "vertex", 0, 0, tiled=True)
        aggregate = jnp.sum(arrived.astype(jnp.float32), axis=0).reshape(picks, width)
        support = (
            (1.0 - RESIDUAL_SHARE) * aggregate + RESIDUAL_SHARE * initial
        ).astype(jnp.bfloat16)
        near = jnp.stack([support] + [rotated(support, "section", by) for by in range(1, layers)])
        gathered = lax.all_gather(near, "feat", axis=0)
        if layer < layers - 1:
            partial = layer_step(
                gathered,
                support,
                slices_ordered[layer],
                statics[layer],
                columns,
                betas[layer],
                row_devices,
            )
        kept = gathered if kept is None else jnp.where(section == layer, gathered, kept)
        if layer < layers - 1:
            kept_before = (
                gathered
                if kept_before is None
                else jnp.where(section == layer + 1, gathered, kept_before)
            )

    def own_columns(array):
        mine = lax.dynamic_index_in_dim(array, feat, 0, keepdims=False)
        mine = jnp.take(mine, order, axis=0)
        return jnp.transpose(mine, (1, 0, 2)).reshape(picks, half)

    beta_rate = jnp.log(BETA_SCALE / (section + 1).astype(jnp.float32) + 1.0)
    beta_before = jnp.log(BETA_SCALE / jnp.maximum(section, 1).astype(jnp.float32) + 1.0)
    rows_before = whole_rows(kept_before, own_columns(kept_before), before_ordered, beta_before)
    fresh = jnp.where(section == 0, initial_half, rows_before)
    placed = jnp.dot(select, fresh, preferred_element_type=jnp.float32).astype(jnp.bfloat16)
    table = jnp.where(upto[spans - 1][:, None], placed, stored)
    rows_out = whole_rows(kept, own_columns(kept), own_ordered, beta_rate)
    return (rows_out.reshape(1, spans, rows_local, half), table[None])


def solution(mesh):
    placed = (
        P("vertex", "feat"),
        P("section", "vertex", "feat"),
        P("section", None, "feat"),
        P(None, "vertex", None, None),
        P(None, "vertex"),
        P(None, "vertex"),
        P(None, "vertex"),
        P(None, "vertex"),
    )
    return jax.shard_map(
        shards,
        mesh=mesh,
        in_specs=placed,
        out_specs=(P("section", None, "vertex", "feat"), P("section", "vertex", "feat")),
        check_vma=False,
    )
```

```python
import math

import jax
import jax.numpy as jnp
from jax import lax
from jax.experimental import pallas as pl
from jax.experimental.pallas import tpu as pltpu
from jax.sharding import PartitionSpec as P

RESIDUAL_SHARE = 0.2
BETA_SCALE = 0.5
MIB = 1 << 20
CHUNKS = ((0, 3),)
ROW_CHUNK = 512


def rotated(array, axis, by):
    devices = lax.axis_size(axis)
    return lax.ppermute(array, axis, [(i, (i + by) % devices) for i in range(devices)])


def after(array, earlier):
    return lax.optimization_barrier((array, earlier))[0]


def vmem_params(mib):
    return pltpu.CompilerParams(vmem_limit_bytes=mib * MIB)


def cost(flops, bytes_accessed):
    return pl.CostEstimate(flops=flops, transcendentals=0, bytes_accessed=bytes_accessed)


def dense_adjacency(tile_values, tile_rows, tile_cols, tile_counts, row_blocks, col_blocks):
    spans, slots, side, _ = tile_values.shape
    rows, cols = row_blocks * side, col_blocks * side

    def kernel(rows_ref, cols_ref, counts_ref, values_ref, out_ref):
        span = pl.program_id(0)
        out_ref[...] = jnp.zeros_like(out_ref)

        @pl.loop(0, counts_ref[span])
        def _(slot):
            row = pl.multiple_of(rows_ref[span, slot] * side, side)
            col = pl.multiple_of(cols_ref[span, slot] * side, side)
            out_ref[0, pl.ds(row, side), pl.ds(col, side)] = values_ref[0, slot]

    return pl.pallas_call(
        kernel,
        out_shape=jax.ShapeDtypeStruct((spans, rows, cols), jnp.bfloat16),
        grid_spec=pltpu.PrefetchScalarGridSpec(
            num_scalar_prefetch=3,
            grid=(spans,),
            in_specs=[pl.BlockSpec((1, slots, side, side), lambda c, *_: (c, 0, 0, 0))],
            out_specs=pl.BlockSpec((1, rows, cols), lambda c, *_: (c, 0, 0)),
        ),
        compiler_params=vmem_params(40),
        cost_estimate=cost(0, 2 * spans * (rows * cols + slots * side * side)),
        name="dense_adjacency",
    )(tile_rows, tile_cols, tile_counts[:, 0], tile_values)


def first_partial(adjacency, hist, feats, replaced, row_devices, begin, end):
    _, rows, cols = adjacency.shape
    spans = end - begin
    width = hist.shape[1]
    rows_local = rows // row_devices
    step = ROW_CHUNK // rows_local

    def kernel(adj_ref, hist_ref, feat_ref, mask_ref, out_ref, table):
        @pl.when(pl.program_id(1) == 0)
        def _():
            table[...] = jnp.where(mask_ref[0] > 0, feat_ref[...], hist_ref[...])

        part = jnp.dot(adj_ref[0], table[...], preferred_element_type=jnp.float32)
        out_ref[:, 0] = part.astype(jnp.bfloat16).reshape(step, rows_local, width)

    return pl.pallas_call(
        kernel,
        out_shape=jax.ShapeDtypeStruct((row_devices, spans, rows_local, width), jnp.bfloat16),
        grid=(spans, rows // ROW_CHUNK),
        in_specs=[
            pl.BlockSpec((1, ROW_CHUNK, cols), lambda c, m: (c + begin, m, 0)),
            pl.BlockSpec((cols, width), lambda c, m: (0, 0)),
            pl.BlockSpec((cols, width), lambda c, m: (0, 0)),
            pl.BlockSpec((1, cols, width), lambda c, m: (c + begin, 0, 0)),
        ],
        out_specs=pl.BlockSpec((step, 1, rows_local, width), lambda c, m: (m, c, 0, 0)),
        scratch_shapes=[pltpu.VMEM((cols, width), jnp.bfloat16)],
        compiler_params=vmem_params(24),
        cost_estimate=cost(
            2 * spans * rows * cols * width, 2 * spans * (rows * cols + rows * width)
        ),
        name="first_partial",
    )(adjacency, hist, feats, replaced)


def replaced_columns(adjacency, select, begin, end):
    _, rows, cols = adjacency.shape
    spans = end - begin
    picks = select.shape[1]

    def kernel(adj_ref, sel_ref, out_ref):
        out_ref[0] = jnp.dot(
            adj_ref[0], sel_ref[...], preferred_element_type=jnp.float32
        ).astype(jnp.bfloat16)

    return pl.pallas_call(
        kernel,
        out_shape=jax.ShapeDtypeStruct((spans, rows, picks), jnp.bfloat16),
        grid=(spans, rows // ROW_CHUNK),
        in_specs=[
            pl.BlockSpec((1, ROW_CHUNK, cols), lambda c, m: (c + begin, m, 0)),
            pl.BlockSpec((cols, picks), lambda c, m: (0, 0)),
        ],
        out_specs=pl.BlockSpec((1, ROW_CHUNK, picks), lambda c, m: (c, m, 0)),
        compiler_params=vmem_params(24),
        cost_estimate=cost(2 * spans * rows * cols * picks, 2 * spans * rows * (cols + picks)),
        name="replaced_columns",
    )(adjacency, select)


def static_parts(adjacency, hist_slices, replaced, begin, end):
    _, rows, cols = adjacency.shape
    spans = end - begin
    layers, _, width = hist_slices.shape
    later = layers - 1

    def kernel(adj_ref, hist_ref, mask_ref, static_ref, right):
        @pl.when(pl.program_id(1) == 0)
        def _():
            for layer in range(later):
                right[:, layer * width : (layer + 1) * width] = jnp.where(
                    mask_ref[0] > 0, jnp.zeros_like(hist_ref[0]), hist_ref[layer + 1]
                )

        part = jnp.dot(adj_ref[0], right[...], preferred_element_type=jnp.float32)
        for layer in range(later):
            static_ref[layer, 0] = part[:, layer * width : (layer + 1) * width]

    return pl.pallas_call(
        kernel,
        out_shape=jax.ShapeDtypeStruct((later, spans, rows, width), jnp.float32),
        grid=(spans, rows // ROW_CHUNK),
        in_specs=[
            pl.BlockSpec((1, ROW_CHUNK, cols), lambda c, m: (c + begin, m, 0)),
            pl.BlockSpec((layers, cols, width), lambda c, m: (0, 0, 0)),
            pl.BlockSpec((1, cols, width), lambda c, m: (c + begin, 0, 0)),
        ],
        out_specs=pl.BlockSpec((later, 1, ROW_CHUNK, width), lambda c, m: (0, c, m, 0)),
        scratch_shapes=[pltpu.VMEM((cols, later * width), jnp.bfloat16)],
        compiler_params=vmem_params(32),
        cost_estimate=cost(
            2 * spans * rows * cols * later * width,
            spans * (2 * rows * cols + 4 * later * rows * width),
        ),
        name="static_parts",
    )(adjacency, hist_slices, replaced)


def fill_left(left, gath_ref, section, halves, parts, width):
    for half in range(halves):
        for part in range(parts):
            first = (half * parts + part) * width
            place = lax.rem(section - part + parts, parts)
            left[:, first : first + width] = gath_ref[half, place]


def layer_step(place, gathered, support, slices, statics, columns, fresh_before, layer, beta, row_devices, begin):
    halves, parts, picks, width = gathered.shape
    spans, rows, every = columns.shape
    rows_local = rows // row_devices
    depth = halves * parts * width
    used_before = begin * rows_local
    step = 4

    def kernel(place_ref, gath_ref, sup_ref, w_ref, static_ref, cols_ref, *refs):
        if begin:
            before_ref, fresh_ref, out_ref, left, known = refs
            known[:used_before] = before_ref[...]
        else:
            fresh_ref, out_ref, left, known = refs
        fill_left(left, gath_ref, place_ref[0], halves, parts, width)
        projected = jnp.dot(left[...], w_ref[0], preferred_element_type=jnp.float32)
        fresh = jnp.maximum(
            (1.0 - beta) * sup_ref[...].astype(jnp.float32) + beta * projected, 0.0
        ).astype(jnp.bfloat16)
        known[used_before:] = fresh
        fresh_ref[...] = known[...]
        for span in range(spans):
            used = (begin + span + 1) * rows_local
            right = known[:used]
            for first in range(0, row_devices, step):
                at = slice(first * rows_local, (first + step) * rows_local)
                part = static_ref[0, span, at] + jnp.dot(
                    cols_ref[span, at, :used], right, preferred_element_type=jnp.float32
                )
                out_ref[first : first + step, span] = part.astype(jnp.bfloat16).reshape(
                    step, rows_local, width
                )

    whole = used_before + picks
    operands = [gathered, support, slices, statics, columns]
    specs = [
        pl.BlockSpec(gathered.shape, lambda i, p: (0, 0, 0, 0)),
        pl.BlockSpec(support.shape, lambda i, p: (0, 0)),
        pl.BlockSpec((1, depth, width), lambda i, p: (lax.rem(p[0] - layer + parts, parts), 0, 0)),
        pl.BlockSpec((1, spans, rows, width), lambda i, p: (layer, 0, 0, 0)),
        pl.BlockSpec(columns.shape, lambda i, p: (0, 0, 0)),
    ]
    if begin:
        operands.append(fresh_before)
        specs.append(pl.BlockSpec(fresh_before.shape, lambda i, p: (0, 0)))
    return pl.pallas_call(
        kernel,
        out_shape=(
            jax.ShapeDtypeStruct((whole, width), jnp.bfloat16),
            jax.ShapeDtypeStruct((row_devices, spans, rows_local, width), jnp.bfloat16),
        ),
        grid_spec=pltpu.PrefetchScalarGridSpec(
            num_scalar_prefetch=1,
            grid=(1,),
            in_specs=specs,
            out_specs=(
                pl.BlockSpec((whole, width), lambda i, p: (0, 0)),
                pl.BlockSpec((row_devices, spans, rows_local, width), lambda i, p: (0, 0, 0, 0)),
            ),
            scratch_shapes=[
                pltpu.VMEM((picks, depth), jnp.bfloat16),
                pltpu.VMEM((whole, width), jnp.bfloat16),
            ],
        ),
        compiler_params=vmem_params(40),
        cost_estimate=cost(
            2 * picks * depth * width + 2 * spans * rows * width * every,
            6 * spans * rows * width + 2 * spans * rows * every,
        ),
        name="layer_step",
    )(place, *operands)


def whole_rows(place, betas, gathered, weight_cols, earlier, layer):
    halves, parts, picks, width = gathered.shape
    depth, half = weight_cols.shape

    def kernel(place_ref, betas_ref, gath_ref, w_ref, *refs):
        if layer:
            earlier_ref, out_ref, left, own = refs
        else:
            out_ref, left, own = refs
        section, feat = place_ref[0], place_ref[1]

        @pl.when(section == layer)
        def _():
            beta = betas_ref[layer]
            fill_left(left, gath_ref, section, halves, parts, width)
            for part in range(parts):
                own[:, part * width : (part + 1) * width] = gath_ref[
                    feat, lax.rem(section - part + parts, parts)
                ]
            projected = jnp.dot(left[...], w_ref[...], preferred_element_type=jnp.float32)
            out_ref[...] = jnp.maximum(
                (1.0 - beta) * own[...].astype(jnp.float32) + beta * projected, 0.0
            ).astype(jnp.bfloat16)

        @pl.when(section != layer)
        def _():
            out_ref[...] = earlier_ref[...] if layer else jnp.zeros_like(out_ref)

    operands = [gathered, weight_cols] + ([earlier] if layer else [])
    specs = [
        pl.BlockSpec(gathered.shape, lambda i, *_: (0, 0, 0, 0)),
        pl.BlockSpec(weight_cols.shape, lambda i, *_: (0, 0)),
    ] + ([pl.BlockSpec((picks, half), lambda i, *_: (0, 0))] if layer else [])
    return pl.pallas_call(
        kernel,
        out_shape=jax.ShapeDtypeStruct((picks, half), jnp.bfloat16),
        grid_spec=pltpu.PrefetchScalarGridSpec(
            num_scalar_prefetch=2,
            grid=(1,),
            in_specs=specs,
            out_specs=pl.BlockSpec((picks, half), lambda i, *_: (0, 0)),
            scratch_shapes=[
                pltpu.VMEM((picks, depth), jnp.bfloat16),
                pltpu.VMEM((picks, half), jnp.bfloat16),
            ],
        ),
        compiler_params=vmem_params(24),
        cost_estimate=cost(2 * picks * depth * half, 2 * (picks * depth + depth * half)),
        name="whole_rows",
    )(place, betas, *operands)


def replace_rows(stored, ids, fresh):
    owned, half = stored.shape
    picks = ids.shape[1]
    chunk = 512

    def kernel(stored_ref, ids_ref, fresh_ref, out_ref):
        first = pl.program_id(0) * chunk
        vertex = first + lax.broadcasted_iota(jnp.int32, (chunk, picks), 0)
        hits = (vertex == ids_ref[...]).astype(jnp.float32)
        placed = jnp.dot(
            hits.astype(jnp.bfloat16), fresh_ref[...], preferred_element_type=jnp.float32
        )
        found = jnp.sum(hits, axis=1, keepdims=True) > 0
        out_ref[...] = jnp.where(found, placed, stored_ref[...].astype(jnp.float32)).astype(
            jnp.bfloat16
        )

    return pl.pallas_call(
        kernel,
        out_shape=jax.ShapeDtypeStruct((owned, half), jnp.bfloat16),
        grid=(owned // chunk,),
        in_specs=[
            pl.BlockSpec((chunk, half), lambda i: (i, 0)),
            pl.BlockSpec((1, picks), lambda i: (0, 0)),
            pl.BlockSpec((picks, half), lambda i: (0, 0)),
        ],
        out_specs=pl.BlockSpec((chunk, half), lambda i: (i, 0)),
        compiler_params=vmem_params(24),
        cost_estimate=cost(2 * owned * picks * half, 4 * owned * half),
        name="replace_rows",
    )(stored, ids, fresh)


def shards(features, history, weights, tile_values, tile_rows, tile_cols, tile_counts, span_ids):
    spans, rows_local = span_ids.shape
    side = tile_values.shape[2]
    owned, half = features.shape
    layers = lax.axis_size("section")
    row_devices = lax.axis_size("vertex")
    section = lax.axis_index("section")
    width = half // layers
    picks = spans * rows_local
    depth = weights.shape[1]
    betas = [math.log(BETA_SCALE / (layer + 1) + 1.0) for layer in range(layers)]
    place = jnp.stack([section, lax.axis_index("feat")]).astype(jnp.int32)
    beta_table = jnp.array(betas, jnp.float32)

    stored = history[0]
    by_section = jnp.stack([stored[:, i * width : (i + 1) * width] for i in range(layers)])
    hist_slices = lax.all_to_all(by_section, "section", 0, 0, tiled=True)

    ids = span_ids.reshape(1, picks)
    hits = jnp.arange(owned)[:, None] == ids
    select = hits.astype(jnp.bfloat16)
    upto = jnp.stack([jnp.any(hits[:, : (c + 1) * rows_local], axis=1) for c in range(spans)])
    replaced = jnp.broadcast_to(upto[:, :, None], (spans, owned, width)).astype(jnp.bfloat16)
    feat_slice = lax.dynamic_slice_in_dim(features, section * width, width, 1)
    initial_half = jnp.take(features, ids[0], axis=0)
    initial = lax.dynamic_slice_in_dim(initial_half, section * width, width, 1).astype(jnp.float32)
    adjacency = dense_adjacency(
        tile_values, tile_rows, tile_cols, tile_counts, rows_local * row_devices // side, owned // side
    )
    columns = [replaced_columns(adjacency, select, begin, end) for begin, end in CHUNKS]

    partials = [
        first_partial(adjacency, hist_slices[0], feat_slice, replaced, row_devices, begin, end)
        for begin, end in CHUNKS
    ]
    own_weights = after(weights[0], partials)
    late_slices = after(hist_slices, partials)
    statics = [static_parts(adjacency, late_slices, replaced, begin, end) for begin, end in CHUNKS]
    by_distance = [
        lax.dynamic_slice_in_dim(own_weights, (section + by) % layers * width, width, 1)
        for by in range(layers)
    ]
    weight_slices = jnp.stack(
        [by_distance[0]] + [rotated(by_distance[by], "section", by) for by in range(1, layers)]
    )

    rows_kept = [None] * len(CHUNKS)
    table = None
    for layer in range(layers):
        fresh = None
        if layer == layers - 1:
            before = rotated(jnp.concatenate(rows_kept, axis=0), "section", 1)
            table = replace_rows(stored, ids, jnp.where(section == 0, initial_half, before))
        for index, (begin, end) in enumerate(CHUNKS):
            mine = slice(begin * rows_local, end * rows_local)
            arrived = lax.all_to_all(partials[index], "vertex", 0, 0, tiled=True)
            if table is not None:
                arrived, table = lax.optimization_barrier((arrived, table))
            aggregate = jnp.sum(arrived.astype(jnp.float32), axis=0).reshape(-1, width)
            support = (
                (1.0 - RESIDUAL_SHARE) * aggregate + RESIDUAL_SHARE * initial[mine]
            ).astype(jnp.bfloat16)
            near = jnp.stack(
                [support] + [rotated(support, "section", by) for by in range(1, layers)]
            )
            gathered = lax.all_gather(near, "feat", axis=0)
            if layer < layers - 1:
                fresh, partials[index] = layer_step(
                    place,
                    gathered,
                    support,
                    weight_slices,
                    statics[index],
                    columns[index],
                    fresh,
                    layer,
                    betas[layer],
                    row_devices,
                    begin,
                )
            rows_kept[index] = whole_rows(
                place, beta_table, gathered, own_weights, rows_kept[index], layer
            )
    rows_out = jnp.concatenate(rows_kept, axis=0)
    return (rows_out.reshape(1, spans, rows_local, half), table[None])


def solution(mesh):
    placed = (
        P("vertex", "feat"),
        P("section", "vertex", "feat"),
        P("section", None, "feat"),
        P(None, "vertex", None, None),
        P(None, "vertex"),
        P(None, "vertex"),
        P(None, "vertex"),
        P(None, "vertex"),
    )
    return jax.shard_map(
        shards,
        mesh=mesh,
        in_specs=placed,
        out_specs=(P("section", None, "vertex", "feat"), P("section", "vertex", "feat")),
        check_vma=False,
    )
```

```python
import math

import jax
import jax.numpy as jnp
from jax import lax
from jax.experimental import pallas as pl
from jax.experimental.pallas import tpu as pltpu
from jax.sharding import PartitionSpec as P

RESIDUAL_SHARE = 0.2
BETA_SCALE = 0.5
MIB = 1 << 20
ROW_CHUNK = 1024
KERNEL_VMEM = 58
IN_HBM = pl.BlockSpec(memory_space=pltpu.HBM)
IN_VMEM = pl.BlockSpec(memory_space=pltpu.VMEM)
IN_SMEM = pl.BlockSpec(memory_space=pltpu.SMEM)


def rotated(array, axis, by):
    devices = lax.axis_size(axis)
    return lax.ppermute(array, axis, [(i, (i + by) % devices) for i in range(devices)])


def after(array, earlier):
    return lax.optimization_barrier((array, earlier))[0]


def vmem_params(mib):
    return pltpu.CompilerParams(vmem_limit_bytes=mib * MIB)


def cost(flops, bytes_accessed):
    return pl.CostEstimate(flops=flops, transcendentals=0, bytes_accessed=bytes_accessed)


def rows_from(tiles_ref, slots_ref, span, first, count, col_blocks):
    lines = []
    for row in range(count):
        base = (first + row) * col_blocks
        lines.append(
            jnp.concatenate(
                [tiles_ref[span, slots_ref[span, base + col]] for col in range(col_blocks)], axis=1
            )
        )
    return jnp.concatenate(lines, axis=0)


def tile_copies(tiles_ref, held, sems):
    spans, slots = tiles_ref.shape[:2]
    return [
        pltpu.make_async_copy(
            tiles_ref.at[span], held.at[span, pl.ds(0, slots)], sems.at[span]
        )
        for span in range(spans)
    ]


def tile_scratch(tiles):
    spans, slots, side, _ = tiles.shape
    return [pltpu.VMEM((spans, slots + 1, side, side), jnp.bfloat16), pltpu.SemaphoreType.DMA((spans,))]


def first_partial(tiles, slots, hist_slices, feats, replaced, row_devices):
    spans, slot_count, side, _ = tiles.shape
    _, cols, width = hist_slices.shape
    col_blocks = cols // side
    row_blocks = slots.shape[1] // col_blocks
    step = ROW_CHUNK // side
    chunks = row_blocks // step

    def kernel(slots_ref, tiles_ref, hist_ref, feat_ref, mask_ref, out_ref, held, tile_sems, hist, hist_sem, table, sums, out_sems):
        hist_copy = pltpu.make_async_copy(hist_ref.at[0], hist, hist_sem)
        copies = tile_copies(tiles_ref, held, tile_sems)
        for copy in [hist_copy] + copies:
            copy.start()
        def sent(span, chunk):
            at = pl.ds(chunk * step, step)
            return pltpu.make_async_copy(
                sums.at[span, at], out_ref.at[at, span], out_sems.at[span, chunk]
            )

        hist_copy.wait()
        for span in range(spans):
            held[span, slot_count] = jnp.zeros((side, side), jnp.bfloat16)
            table[...] = jnp.where(mask_ref[span] > 0, feat_ref[...], hist[...])
            copies[span].wait()

            @pl.loop(0, chunks)
            def _(chunk):
                left = rows_from(held, slots_ref, span, chunk * step, step, col_blocks)
                part = jnp.dot(left, table[...], preferred_element_type=jnp.float32)
                sums[span, pl.ds(chunk * step, step)] = part.astype(jnp.bfloat16).reshape(
                    step, side, width
                )
                sent(span, chunk).start()

        for span in range(spans):
            for chunk in range(chunks):
                sent(span, chunk).wait()

    return pl.pallas_call(
        kernel,
        out_shape=jax.ShapeDtypeStruct((row_devices, spans, side, width), jnp.bfloat16),
        in_specs=[IN_SMEM, IN_HBM, IN_HBM, IN_VMEM, IN_VMEM],
        out_specs=IN_HBM,
        scratch_shapes=[
            *tile_scratch(tiles),
            pltpu.VMEM((cols, width), jnp.bfloat16),
            pltpu.SemaphoreType.DMA(()),
            pltpu.VMEM((cols, width), jnp.bfloat16),
            pltpu.VMEM((spans, row_devices, side, width), jnp.bfloat16),
            pltpu.SemaphoreType.DMA((spans, chunks)),
        ],
        compiler_params=vmem_params(KERNEL_VMEM),
        cost_estimate=cost(2 * spans * row_blocks * side * cols * width, 2 * tiles.size),
        name="first_partial",
    )(slots, tiles, hist_slices, feats, replaced)


def section_slices(array, parts):
    rows, cols = array.shape
    width = cols // parts
    step = rows // 4

    def kernel(in_ref, out_ref):
        for part in range(parts):
            out_ref[part] = in_ref[:, part * width : (part + 1) * width]

    return pl.pallas_call(
        kernel,
        out_shape=jax.ShapeDtypeStruct((parts, rows, width), array.dtype),
        grid=(rows // step,),
        in_specs=[pl.BlockSpec((step, cols), lambda i: (i, 0))],
        out_specs=pl.BlockSpec((parts, step, width), lambda i: (0, i, 0)),
        compiler_params=vmem_params(KERNEL_VMEM),
        cost_estimate=cost(0, 4 * rows * cols),
        name="section_slices",
    )(array)


def selection(ids, owned, width):
    spans, rows_local = ids.shape
    picks = spans * rows_local
    chunk = 512

    def kernel(ids_ref, select_ref, mask_ref):
        first = pl.program_id(0) * chunk
        vertex = first + lax.broadcasted_iota(jnp.int32, (chunk, picks), 0)
        hits = (vertex == ids_ref[...]).astype(jnp.float32)
        select_ref[...] = hits.astype(jnp.bfloat16)
        total = jnp.zeros((chunk, 1), jnp.float32)
        for span in range(spans):
            part = hits[:, span * rows_local : (span + 1) * rows_local]
            total = total + jnp.sum(part, axis=1, keepdims=True)
            mask_ref[span] = jnp.broadcast_to(total, (chunk, width)).astype(jnp.bfloat16)

    return pl.pallas_call(
        kernel,
        out_shape=(
            jax.ShapeDtypeStruct((owned, picks), jnp.bfloat16),
            jax.ShapeDtypeStruct((spans, owned, width), jnp.bfloat16),
        ),
        grid=(owned // chunk,),
        in_specs=[pl.BlockSpec((1, picks), lambda i: (0, 0))],
        out_specs=(
            pl.BlockSpec((chunk, picks), lambda i: (i, 0)),
            pl.BlockSpec((spans, chunk, width), lambda i: (0, i, 0)),
        ),
        compiler_params=vmem_params(16),
        cost_estimate=cost(owned * picks, 4 * owned * picks),
        name="selection",
    )(ids.reshape(1, picks))


def collect(arrived, initial):
    owners, spans, rows_local, width = arrived.shape

    groups = 4
    each = owners // groups

    def kernel(in_ref, init_ref, out_ref, held, sems, sums):
        copies = [
            pltpu.make_async_copy(
                in_ref.at[pl.ds(group * each, each)], held.at[pl.ds(group * each, each)], sems.at[group]
            )
            for group in range(groups)
        ]
        for copy in copies:
            copy.start()
        for group in range(groups):
            copies[group].wait()
            for span in range(spans):
                at = slice(span * rows_local, (span + 1) * rows_local)
                total = held[group * each, span].astype(jnp.float32)
                for owner in range(group * each + 1, (group + 1) * each):
                    total = total + held[owner, span].astype(jnp.float32)
                if group:
                    total = sums[at] + total
                if group < groups - 1:
                    sums[at] = total
                else:
                    out_ref[at] = (
                        (1.0 - RESIDUAL_SHARE) * total + RESIDUAL_SHARE * init_ref[at]
                    ).astype(jnp.bfloat16)

    return pl.pallas_call(
        kernel,
        out_shape=jax.ShapeDtypeStruct((spans * rows_local, width), jnp.bfloat16),
        in_specs=[IN_HBM, IN_VMEM],
        out_specs=IN_VMEM,
        scratch_shapes=[
            pltpu.VMEM(arrived.shape, jnp.bfloat16),
            pltpu.SemaphoreType.DMA((groups,)),
            pltpu.VMEM((spans * rows_local, width), jnp.float32),
        ],
        compiler_params=vmem_params(16),
        cost_estimate=cost(arrived.size, 2 * arrived.size),
        name="collect",
    )(arrived, initial)


def static_parts(tiles, slots, hist_slices, replaced, select, which):
    spans, slot_count, side, _ = tiles.shape
    layers, cols, width = hist_slices.shape
    col_blocks = cols // side
    row_blocks = slots.shape[1] // col_blocks
    rows = row_blocks * side
    with_columns = which[0] == 1
    rows_local = select.shape[1] // spans
    picks = select.shape[1] if with_columns else 0
    kinds = len(which)
    stored = kinds * width
    step = ROW_CHUNK // side
    chunks = row_blocks // step

    def kernel(slots_ref, tiles_ref, hist_ref, mask_ref, sel_ref, *refs):
        static_refs = refs[:kinds]
        column_refs = refs[kinds : kinds + (spans if with_columns else 0)]
        held, tile_sems, hist, hist_sems, right, sums, sums_sems, cols_held, cols_sems = refs[-9:]
        hist_copies = [
            pltpu.make_async_copy(hist_ref.at[layer], hist.at[index], hist_sems.at[index])
            for index, layer in enumerate(which)
        ]
        copies = tile_copies(tiles_ref, held, tile_sems)
        for copy in hist_copies + copies:
            copy.start()
        if with_columns:
            right[:, stored:] = sel_ref[...]
        for copy in hist_copies:
            copy.wait()
        def sent(span, chunk, used):
            at = pl.ds(pl.multiple_of(chunk * ROW_CHUNK, ROW_CHUNK), ROW_CHUNK)
            moves = [
                pltpu.make_async_copy(
                    sums.at[index, span, at],
                    static_refs[index].at[span, at],
                    sums_sems.at[index, span, chunk],
                )
                for index in range(kinds)
            ]
            if with_columns:
                moves.append(
                    pltpu.make_async_copy(
                        cols_held.at[span, at, pl.ds(0, used)],
                        column_refs[span].at[at],
                        cols_sems.at[span, chunk],
                    )
                )
            return moves

        for span in range(spans):
            held[span, slot_count] = jnp.zeros((side, side), jnp.bfloat16)
            for index in range(kinds):
                right[:, index * width : (index + 1) * width] = jnp.where(
                    mask_ref[span] > 0, jnp.zeros_like(hist[index]), hist[index]
                )
            used = (span + 1) * rows_local if with_columns else 0
            copies[span].wait()

            @pl.loop(0, chunks)
            def _(chunk):
                left = rows_from(held, slots_ref, span, chunk * step, step, col_blocks)
                part = jnp.dot(
                    left, right[:, : stored + used], preferred_element_type=jnp.float32
                )
                at = pl.ds(pl.multiple_of(chunk * ROW_CHUNK, ROW_CHUNK), ROW_CHUNK)
                for index in range(kinds):
                    sums[index, span, at] = part[:, index * width : (index + 1) * width]
                if with_columns:
                    cols_held[span, at, :used] = part[:, stored:].astype(jnp.bfloat16)
                for move in sent(span, chunk, used):
                    move.start()

        for span in range(spans):
            for chunk in range(chunks):
                for move in sent(span, chunk, (span + 1) * rows_local):
                    move.wait()

    out_shape = [jax.ShapeDtypeStruct((spans, rows, width), jnp.float32) for _ in which]
    if with_columns:
        out_shape += [
            jax.ShapeDtypeStruct((rows, (span + 1) * rows_local), jnp.bfloat16)
            for span in range(spans)
        ]
    return pl.pallas_call(
        kernel,
        out_shape=tuple(out_shape),
        in_specs=[IN_SMEM, IN_HBM, IN_HBM, IN_VMEM, IN_VMEM],
        out_specs=tuple([IN_HBM] * len(out_shape)),
        scratch_shapes=[
            *tile_scratch(tiles),
            pltpu.VMEM((kinds, cols, width), jnp.bfloat16),
            pltpu.SemaphoreType.DMA((kinds,)),
            pltpu.VMEM((cols, stored + picks), jnp.bfloat16),
            pltpu.VMEM((kinds, spans, rows, width), jnp.float32),
            pltpu.SemaphoreType.DMA((kinds, spans, chunks)),
            pltpu.VMEM((spans, rows, picks) if with_columns else (1, 16, 128), jnp.bfloat16),
            pltpu.SemaphoreType.DMA((spans, chunks)),
        ],
        compiler_params=vmem_params(KERNEL_VMEM),
        cost_estimate=cost(
            2 * spans * rows * cols * (stored + picks),
            2 * tiles.size + spans * (4 * rows * stored + 2 * rows * picks),
        ),
        name="static_parts",
    )(slots, tiles, hist_slices, replaced, select)


def fill_left(left, gath_ref, section, halves, parts, width):
    for half in range(halves):
        for part in range(parts):
            first = (half * parts + part) * width
            place = lax.rem(section - part + parts, parts)
            left[:, first : first + width] = gath_ref[half, place]


def layer_step(place, gathered, support, slices, static, columns, layer, beta, row_devices):
    halves, parts, picks, width = gathered.shape
    spans, rows, _ = static.shape
    rows_local = rows // row_devices
    depth = halves * parts * width
    step = ROW_CHUNK // rows_local
    chunks = row_devices // step

    def kernel(place_ref, gath_ref, sup_ref, static_ref, *refs):
        slice_refs, column_refs = refs[:parts], refs[parts : parts + spans]
        out_ref, left, left_sems, sup, sup_sem, right, right_sem, stat, stat_sems, cols_sems, sums, out_sems = refs[parts + spans : -spans]
        cols = refs[-spans:]
        section = place_ref[0]
        apart = lax.rem(section - layer + parts, parts)
        incoming = []
        for half in range(halves):
            for part in range(parts):
                first = (half * parts + part) * width
                incoming.append(
                    pltpu.make_async_copy(
                        gath_ref.at[half, lax.rem(section - part + parts, parts)],
                        left.at[:, first : first + width],
                        left_sems.at[half, part],
                    )
                )
        incoming.append(pltpu.make_async_copy(sup_ref, sup, sup_sem))
        for copy in incoming:
            copy.start()
        for by in range(parts):
            @pl.when(apart == by)
            def _():
                pltpu.make_async_copy(slice_refs[by], right, right_sem).start()

        later = []
        for span in range(spans):
            pair = (
                pltpu.make_async_copy(column_refs[span], cols[span], cols_sems.at[span]),
                pltpu.make_async_copy(static_ref.at[span], stat.at[span], stat_sems.at[span]),
            )
            for copy in pair:
                copy.start()
            later.append(pair)
        for copy in incoming:
            copy.wait()
        pltpu.make_async_copy(slice_refs[0], right, right_sem).wait()
        projected = jnp.dot(left[...], right[...], preferred_element_type=jnp.float32)
        fresh = jnp.maximum(
            (1.0 - beta) * sup[...].astype(jnp.float32) + beta * projected, 0.0
        ).astype(jnp.bfloat16)
        outgoing = []
        for span in range(spans):
            used = (span + 1) * rows_local
            for copy in later[span]:
                copy.wait()
            for chunk in range(chunks):
                first = chunk * step
                at = slice(chunk * ROW_CHUNK, (chunk + 1) * ROW_CHUNK)
                part = stat[span, at] + jnp.dot(
                    cols[span][at], fresh[:used], preferred_element_type=jnp.float32
                )
                sums[span, first : first + step] = part.astype(jnp.bfloat16).reshape(
                    step, rows_local, width
                )
                outgoing.append(
                    pltpu.make_async_copy(
                        sums.at[span, first : first + step],
                        out_ref.at[first : first + step, span],
                        out_sems.at[span, chunk],
                    )
                )
                outgoing[-1].start()
        for copy in outgoing:
            copy.wait()

    return pl.pallas_call(
        kernel,
        out_shape=jax.ShapeDtypeStruct((row_devices, spans, rows_local, width), jnp.bfloat16),
        in_specs=[IN_SMEM] + [IN_HBM] * (3 + parts + spans),
        out_specs=IN_HBM,
        scratch_shapes=[
            pltpu.VMEM((picks, depth), jnp.bfloat16),
            pltpu.SemaphoreType.DMA((halves, parts)),
            pltpu.VMEM((picks, width), jnp.bfloat16),
            pltpu.SemaphoreType.DMA(()),
            pltpu.VMEM((depth, width), jnp.bfloat16),
            pltpu.SemaphoreType.DMA(()),
            pltpu.VMEM(static.shape, jnp.float32),
            pltpu.SemaphoreType.DMA((spans,)),
            pltpu.SemaphoreType.DMA((spans,)),
            pltpu.VMEM((spans, row_devices, rows_local, width), jnp.bfloat16),
            pltpu.SemaphoreType.DMA((spans, chunks)),
            *[pltpu.VMEM(each.shape, jnp.bfloat16) for each in columns],
        ],
        compiler_params=vmem_params(KERNEL_VMEM),
        cost_estimate=cost(
            2 * picks * depth * width + 2 * spans * rows * width * picks,
            6 * spans * rows * width + 2 * spans * rows * picks,
        ),
        name="layer_step",
    )(place, gathered, support, static, *slices, *columns)


def whole_rows(place, betas, gathered, weight_cols, earlier, layer):
    halves, parts, picks, width = gathered.shape
    depth, half = weight_cols.shape

    def kernel(place_ref, betas_ref, gath_ref, w_ref, *refs):
        if layer:
            earlier_ref, out_ref, left, own = refs
        else:
            out_ref, left, own = refs
        section, feat = place_ref[0], place_ref[1]

        @pl.when(section == layer)
        def _():
            beta = betas_ref[layer]
            fill_left(left, gath_ref, section, halves, parts, width)
            for part in range(parts):
                own[:, part * width : (part + 1) * width] = gath_ref[
                    feat, lax.rem(section - part + parts, parts)
                ]
            projected = jnp.dot(left[...], w_ref[...], preferred_element_type=jnp.float32)
            out_ref[...] = jnp.maximum(
                (1.0 - beta) * own[...].astype(jnp.float32) + beta * projected, 0.0
            ).astype(jnp.bfloat16)

        @pl.when(section != layer)
        def _():
            out_ref[...] = earlier_ref[...] if layer else jnp.zeros_like(out_ref)

    operands = [gathered, weight_cols] + ([earlier] if layer else [])
    return pl.pallas_call(
        kernel,
        out_shape=jax.ShapeDtypeStruct((picks, half), jnp.bfloat16),
        in_specs=[pl.BlockSpec(memory_space=pltpu.SMEM)] * 2
        + [pl.BlockSpec(memory_space=pltpu.VMEM)] * len(operands),
        scratch_shapes=[
            pltpu.VMEM((picks, depth), jnp.bfloat16),
            pltpu.VMEM((picks, half), jnp.bfloat16),
        ],
        compiler_params=vmem_params(16),
        cost_estimate=cost(2 * picks * depth * half, 2 * (picks * depth + depth * half)),
        name="whole_rows",
    )(place, betas, *operands)


def replace_rows(stored, ids, fresh):
    owned, half = stored.shape
    picks = ids.shape[1]
    chunk = 512

    def kernel(stored_ref, ids_ref, fresh_ref, out_ref):
        first = pl.program_id(0) * chunk
        vertex = first + lax.broadcasted_iota(jnp.int32, (chunk, picks), 0)
        hits = (vertex == ids_ref[...]).astype(jnp.float32)
        placed = jnp.dot(
            hits.astype(jnp.bfloat16), fresh_ref[...], preferred_element_type=jnp.float32
        )
        found = jnp.sum(hits, axis=1, keepdims=True) > 0
        out_ref[...] = jnp.where(found, placed, stored_ref[...].astype(jnp.float32)).astype(
            jnp.bfloat16
        )

    return pl.pallas_call(
        kernel,
        out_shape=jax.ShapeDtypeStruct((owned, half), jnp.bfloat16),
        grid=(owned // chunk,),
        in_specs=[
            pl.BlockSpec((chunk, half), lambda i: (i, 0)),
            pl.BlockSpec((1, picks), lambda i: (0, 0)),
            pl.BlockSpec((picks, half), lambda i: (0, 0)),
        ],
        out_specs=pl.BlockSpec((chunk, half), lambda i: (i, 0)),
        compiler_params=vmem_params(24),
        cost_estimate=cost(2 * owned * picks * half, 4 * owned * half),
        name="replace_rows",
    )(stored, ids, fresh)


def shards(features, history, weights, tile_values, tile_rows, tile_cols, tile_counts, span_ids):
    spans, rows_local = span_ids.shape
    side = tile_values.shape[2]
    owned, half = features.shape
    layers = lax.axis_size("section")
    row_devices = lax.axis_size("vertex")
    section = lax.axis_index("section")
    width = half // layers
    picks = spans * rows_local
    depth = weights.shape[1]
    betas = [math.log(BETA_SCALE / (layer + 1) + 1.0) for layer in range(layers)]
    place = jnp.stack([section, lax.axis_index("feat")]).astype(jnp.int32)
    beta_table = jnp.array(betas, jnp.float32)

    stored = history[0]
    hist_slices = lax.all_to_all(section_slices(stored, layers), "section", 0, 0, tiled=True)

    select, replaced = selection(span_ids, owned, width)
    ids = span_ids.reshape(1, picks)
    feat_slice = lax.dynamic_slice_in_dim(features, section * width, width, 1)
    initial_half = jnp.take(features, ids[0], axis=0)
    initial = lax.dynamic_slice_in_dim(initial_half, section * width, width, 1).astype(jnp.float32)
    col_blocks = owned // side
    blocks = rows_local * row_devices // side * col_blocks
    slot_count = tile_rows.shape[1]
    listed = jnp.arange(slot_count)[None, :]
    key = jnp.where(listed < tile_counts, tile_rows * col_blocks + tile_cols, blocks)
    here = key[:, :, None] == jnp.arange(blocks)[None, None, :]
    slots = slot_count + jnp.sum(
        jnp.where(here, listed[:, :, None] - slot_count, 0), axis=1, dtype=jnp.int32
    )
    hist_slices, replaced, feat_slice, initial, slots, select = lax.optimization_barrier(
        (hist_slices, replaced, feat_slice, initial, slots, select)
    )
    partial = first_partial(tile_values, slots, hist_slices, feat_slice, replaced, row_devices)
    own_weights = after(weights[0], partial)
    statics_one, *columns = static_parts(
        tile_values, slots, after(hist_slices, partial), replaced, select, (1,)
    )
    statics = [statics_one]
    by_distance = [
        lax.dynamic_slice_in_dim(own_weights, (section + by) % layers * width, width, 1)
        for by in range(layers)
    ]
    weight_slices = [by_distance[0]] + [
        rotated(by_distance[by], "section", by) for by in range(1, layers)
    ]

    rows_kept = table = None
    for layer in range(layers):
        if layer == layers - 1:
            before = rotated(rows_kept, "section", 1)
            table = replace_rows(stored, ids, jnp.where(section == 0, initial_half, before))
        arrived = lax.all_to_all(partial, "vertex", 0, 0, tiled=True)
        if layer == 0:
            arrived, statics, columns, weight_slices = lax.optimization_barrier(
                (arrived, statics, columns, weight_slices)
            )
        if layer == 1:
            statics += static_parts(
                tile_values,
                slots,
                after(hist_slices, partial),
                replaced,
                select,
                tuple(range(2, layers)),
            )
            arrived, statics = lax.optimization_barrier((arrived, statics))
        if table is not None:
            arrived, table = lax.optimization_barrier((arrived, table))
        support = collect(arrived, initial)
        near = jnp.stack([support] + [rotated(support, "section", by) for by in range(1, layers)])
        gathered = lax.all_gather(near, "feat", axis=0)
        if layer < layers - 1:
            partial = layer_step(
                place,
                gathered,
                support,
                weight_slices,
                statics[layer],
                columns,
                layer,
                betas[layer],
                row_devices,
            )
        rows_kept = whole_rows(place, beta_table, gathered, own_weights, rows_kept, layer)
    return (rows_kept.reshape(1, spans, rows_local, half), table[None])


def solution(mesh):
    placed = (
        P("vertex", "feat"),
        P("section", "vertex", "feat"),
        P("section", None, "feat"),
        P(None, "vertex", None, None),
        P(None, "vertex"),
        P(None, "vertex"),
        P(None, "vertex"),
        P(None, "vertex"),
    )
    return jax.shard_map(
        shards,
        mesh=mesh,
        in_specs=placed,
        out_specs=(P("section", None, "vertex", "feat"), P("section", "vertex", "feat")),
        check_vma=False,
    )
```

```python
import math

import jax
import jax.numpy as jnp
from jax import lax
from jax.experimental import pallas as pl
from jax.experimental.pallas import tpu as pltpu
from jax.sharding import PartitionSpec as P

RESIDUAL_SHARE = 0.2
BETA_SCALE = 0.5
MIB = 1 << 20
ROW_CHUNK = 1024
KERNEL_VMEM = 58
IN_HBM = pl.BlockSpec(memory_space=pltpu.HBM)
IN_VMEM = pl.BlockSpec(memory_space=pltpu.VMEM)
IN_SMEM = pl.BlockSpec(memory_space=pltpu.SMEM)


def rotated(array, axis, by):
    devices = lax.axis_size(axis)
    return lax.ppermute(array, axis, [(i, (i + by) % devices) for i in range(devices)])


def after(array, earlier):
    return lax.optimization_barrier((array, earlier))[0]


def vmem_params(mib):
    return pltpu.CompilerParams(vmem_limit_bytes=mib * MIB)


def cost(flops, bytes_accessed):
    return pl.CostEstimate(flops=flops, transcendentals=0, bytes_accessed=bytes_accessed)


def rows_from(tiles_ref, slots_ref, span, first, count, col_blocks):
    lines = []
    for row in range(count):
        base = (first + row) * col_blocks
        lines.append(
            jnp.concatenate(
                [tiles_ref[span, slots_ref[span, base + col]] for col in range(col_blocks)], axis=1
            )
        )
    return jnp.concatenate(lines, axis=0)


def multiply(tiles_ref, slots_ref, span, right, width, put):
    side = tiles_ref.shape[-1]
    col_blocks = right.shape[0] // side
    row_blocks = slots_ref.shape[1] // col_blocks
    step = ROW_CHUNK // side

    @pl.loop(0, row_blocks, step=step)
    def _(first):
        left = rows_from(tiles_ref, slots_ref, span, first, step, col_blocks)
        part = jnp.dot(left, right[:, :width], preferred_element_type=jnp.float32)
        put(pl.ds(pl.multiple_of(first * side, side), ROW_CHUNK), part)


def tile_copies(tiles_ref, held, sems):
    spans, slots = tiles_ref.shape[:2]
    return [
        pltpu.make_async_copy(
            tiles_ref.at[span], held.at[span, pl.ds(0, slots)], sems.at[span]
        )
        for span in range(spans)
    ]


def tile_scratch(tiles):
    spans, slots, side, _ = tiles.shape
    return [pltpu.VMEM((spans, slots + 1, side, side), jnp.bfloat16), pltpu.SemaphoreType.DMA((spans,))]


def first_partial(tiles, slots, hist_slices, feats, replaced, row_devices):
    spans, slot_count, side, _ = tiles.shape
    _, cols, width = hist_slices.shape
    col_blocks = cols // side
    row_blocks = slots.shape[1] // col_blocks

    def kernel(slots_ref, tiles_ref, hist_ref, feat_ref, mask_ref, out_ref, static_ref, held, tile_sems, hist, hist_sem, table, sums, out_sems, static, static_sems):
        hist_copy = pltpu.make_async_copy(hist_ref.at[pl.ds(0, 2)], hist, hist_sem)
        copies = tile_copies(tiles_ref, held, tile_sems)
        for copy in [hist_copy] + copies:
            copy.start()
        hist_copy.wait()
        outgoing = []
        for span in range(spans):
            held[span, slot_count] = jnp.zeros((side, side), jnp.bfloat16)
            replaces = mask_ref[span] > 0
            table[:, :width] = jnp.where(replaces, feat_ref[...], hist[0])
            table[:, width:] = jnp.where(replaces, jnp.zeros_like(hist[1]), hist[1])
            copies[span].wait()

            def put(at, part, span=span):
                sums[span, at] = part[:, :width].astype(jnp.bfloat16)
                static[span, at] = part[:, width:]

            multiply(held, slots_ref, span, table, 2 * width, put)
            outgoing.append(
                pltpu.make_async_copy(static.at[span], static_ref.at[span], static_sems.at[span])
            )
            outgoing[-1].start()
            for device in range(row_devices):
                outgoing.append(
                    pltpu.make_async_copy(
                        sums.at[span, pl.ds(device * side, side)],
                        out_ref.at[device, span],
                        out_sems.at[span, device],
                    )
                )
                outgoing[-1].start()
        for copy in outgoing:
            copy.wait()

    return pl.pallas_call(
        kernel,
        out_shape=(
            jax.ShapeDtypeStruct((row_devices, spans, side, width), jnp.bfloat16),
            jax.ShapeDtypeStruct((spans, row_blocks * side, width), jnp.float32),
        ),
        in_specs=[IN_SMEM, IN_HBM, IN_HBM, IN_VMEM, IN_VMEM],
        out_specs=(IN_HBM, IN_HBM),
        scratch_shapes=[
            *tile_scratch(tiles),
            pltpu.VMEM((2, cols, width), jnp.bfloat16),
            pltpu.SemaphoreType.DMA(()),
            pltpu.VMEM((cols, 2 * width), jnp.bfloat16),
            pltpu.VMEM((spans, row_blocks * side, width), jnp.bfloat16),
            pltpu.SemaphoreType.DMA((spans, row_devices)),
            pltpu.VMEM((spans, row_blocks * side, width), jnp.float32),
            pltpu.SemaphoreType.DMA((spans,)),
        ],
        compiler_params=vmem_params(KERNEL_VMEM),
        cost_estimate=cost(4 * spans * row_blocks * side * cols * width, 2 * tiles.size),
        name="first_partial",
    )(slots, tiles, hist_slices, feats, replaced)


def section_slices(array, parts):
    rows, cols = array.shape
    width = cols // parts
    groups = 2
    each = rows // groups

    def kernel(in_ref, out_ref, held, in_sems, out_sems):
        moves = []
        for group in range(groups):
            at = pl.ds(group * each, each)
            for part in range(parts):
                moves.append(
                    (
                        pltpu.make_async_copy(
                            in_ref.at[at, pl.ds(part * width, width)],
                            held.at[part, at],
                            in_sems.at[part, group],
                        ),
                        pltpu.make_async_copy(
                            held.at[part, at], out_ref.at[part, at], out_sems.at[part, group]
                        ),
                    )
                )
        for first, _ in moves:
            first.start()
        for first, second in moves:
            first.wait()
            second.start()
        for _, second in moves:
            second.wait()

    return pl.pallas_call(
        kernel,
        out_shape=jax.ShapeDtypeStruct((parts, rows, width), array.dtype),
        in_specs=[IN_HBM],
        out_specs=IN_HBM,
        scratch_shapes=[
            pltpu.VMEM((parts, rows, width), array.dtype),
            pltpu.SemaphoreType.DMA((parts, groups)),
            pltpu.SemaphoreType.DMA((parts, groups)),
        ],
        compiler_params=vmem_params(KERNEL_VMEM),
        cost_estimate=cost(0, 4 * rows * cols),
        name="section_slices",
    )(array)


def selection(ids, owned, width):
    spans, rows_local = ids.shape
    picks = spans * rows_local
    chunk = 512

    def kernel(ids_ref, select_ref, mask_ref):
        first = pl.program_id(0) * chunk
        vertex = first + lax.broadcasted_iota(jnp.int32, (chunk, picks), 0)
        hits = (vertex == ids_ref[...]).astype(jnp.float32)
        select_ref[...] = hits.astype(jnp.bfloat16)
        total = jnp.zeros((chunk, 1), jnp.float32)
        for span in range(spans):
            part = hits[:, span * rows_local : (span + 1) * rows_local]
            total = total + jnp.sum(part, axis=1, keepdims=True)
            mask_ref[span] = jnp.broadcast_to(total, (chunk, width)).astype(jnp.bfloat16)

    return pl.pallas_call(
        kernel,
        out_shape=(
            jax.ShapeDtypeStruct((owned, picks), jnp.bfloat16),
            jax.ShapeDtypeStruct((spans, owned, width), jnp.bfloat16),
        ),
        grid=(owned // chunk,),
        in_specs=[pl.BlockSpec((1, picks), lambda i: (0, 0))],
        out_specs=(
            pl.BlockSpec((chunk, picks), lambda i: (i, 0)),
            pl.BlockSpec((spans, chunk, width), lambda i: (0, i, 0)),
        ),
        compiler_params=vmem_params(16),
        cost_estimate=cost(owned * picks, 4 * owned * picks),
        name="selection",
    )(ids.reshape(1, picks))


def collect(arrived, initial):
    owners, spans, rows_local, width = arrived.shape

    groups = 4
    each = owners // groups

    def kernel(in_ref, init_ref, out_ref, held, sems, sums):
        copies = [
            pltpu.make_async_copy(
                in_ref.at[pl.ds(group * each, each)], held.at[pl.ds(group * each, each)], sems.at[group]
            )
            for group in range(groups)
        ]
        for copy in copies:
            copy.start()
        for group in range(groups):
            copies[group].wait()
            for span in range(spans):
                at = slice(span * rows_local, (span + 1) * rows_local)
                total = held[group * each, span].astype(jnp.float32)
                for owner in range(group * each + 1, (group + 1) * each):
                    total = total + held[owner, span].astype(jnp.float32)
                if group:
                    total = sums[at] + total
                if group < groups - 1:
                    sums[at] = total
                else:
                    out_ref[at] = (
                        (1.0 - RESIDUAL_SHARE) * total + RESIDUAL_SHARE * init_ref[at]
                    ).astype(jnp.bfloat16)

    return pl.pallas_call(
        kernel,
        out_shape=jax.ShapeDtypeStruct((spans * rows_local, width), jnp.bfloat16),
        in_specs=[IN_HBM, IN_VMEM],
        out_specs=IN_VMEM,
        scratch_shapes=[
            pltpu.VMEM(arrived.shape, jnp.bfloat16),
            pltpu.SemaphoreType.DMA((groups,)),
            pltpu.VMEM((spans * rows_local, width), jnp.float32),
        ],
        compiler_params=vmem_params(16),
        cost_estimate=cost(arrived.size, 2 * arrived.size),
        name="collect",
    )(arrived, initial)


def replaced_columns(tiles, slots, select):
    spans, slot_count, side, _ = tiles.shape
    cols, picks = select.shape
    rows = slots.shape[1] // (cols // side) * side
    rows_local = picks // spans

    def kernel(slots_ref, tiles_ref, sel_ref, *refs):
        column_refs, (held, tile_sems, sends) = refs[:spans], refs[spans : spans + 3]
        kept = refs[spans + 3 :]
        copies = tile_copies(tiles_ref, held, tile_sems)
        for copy in copies:
            copy.start()
        outgoing = []
        for span in range(spans):
            used = (span + 1) * rows_local
            held[span, slot_count] = jnp.zeros((side, side), jnp.bfloat16)
            copies[span].wait()

            def put(at, part, span=span):
                kept[span][at] = part.astype(jnp.bfloat16)

            multiply(held, slots_ref, span, sel_ref, used, put)
            outgoing.append(pltpu.make_async_copy(kept[span], column_refs[span], sends.at[span]))
            outgoing[-1].start()
        for copy in outgoing:
            copy.wait()

    shapes = [(rows, (span + 1) * rows_local) for span in range(spans)]
    return pl.pallas_call(
        kernel,
        out_shape=tuple(jax.ShapeDtypeStruct(shape, jnp.bfloat16) for shape in shapes),
        in_specs=[IN_SMEM, IN_HBM, IN_VMEM],
        out_specs=(IN_HBM,) * spans,
        scratch_shapes=[
            *tile_scratch(tiles),
            pltpu.SemaphoreType.DMA((spans,)),
            *[pltpu.VMEM(shape, jnp.bfloat16) for shape in shapes],
        ],
        compiler_params=vmem_params(KERNEL_VMEM),
        cost_estimate=cost(2 * spans * rows * cols * picks, 2 * tiles.size + 6 * rows * picks),
        name="replaced_columns",
    )(slots, tiles, select)


def static_parts(tiles, slots, hist_slices, replaced):
    spans, slot_count, side, _ = tiles.shape
    layers, cols, width = hist_slices.shape
    rows = slots.shape[1] // (cols // side) * side
    kinds = layers - 2
    stored = kinds * width

    def kernel(slots_ref, tiles_ref, hist_ref, mask_ref, *refs):
        static_refs = refs[:kinds]
        held, tile_sems, hist, hist_sem, right, sums, sends = refs[kinds:]
        hist_copy = pltpu.make_async_copy(hist_ref.at[pl.ds(2, kinds)], hist, hist_sem)
        copies = tile_copies(tiles_ref, held, tile_sems)
        for copy in [hist_copy] + copies:
            copy.start()
        hist_copy.wait()
        outgoing = []
        for span in range(spans):
            held[span, slot_count] = jnp.zeros((side, side), jnp.bfloat16)
            for index in range(kinds):
                right[:, index * width : (index + 1) * width] = jnp.where(
                    mask_ref[span] > 0, jnp.zeros_like(hist[index]), hist[index]
                )
            copies[span].wait()

            def put(at, part, span=span):
                for index in range(kinds):
                    sums[index, span, at] = part[:, index * width : (index + 1) * width]

            multiply(held, slots_ref, span, right, stored, put)
            for index in range(kinds):
                outgoing.append(
                    pltpu.make_async_copy(
                        sums.at[index, span], static_refs[index].at[span], sends.at[index, span]
                    )
                )
                outgoing[-1].start()
        for copy in outgoing:
            copy.wait()

    return pl.pallas_call(
        kernel,
        out_shape=(jax.ShapeDtypeStruct((spans, rows, width), jnp.float32),) * kinds,
        in_specs=[IN_SMEM, IN_HBM, IN_HBM, IN_VMEM],
        out_specs=(IN_HBM,) * kinds,
        scratch_shapes=[
            *tile_scratch(tiles),
            pltpu.VMEM((kinds, cols, width), jnp.bfloat16),
            pltpu.SemaphoreType.DMA(()),
            pltpu.VMEM((cols, stored), jnp.bfloat16),
            pltpu.VMEM((kinds, spans, rows, width), jnp.float32),
            pltpu.SemaphoreType.DMA((kinds, spans)),
        ],
        compiler_params=vmem_params(KERNEL_VMEM),
        cost_estimate=cost(
            2 * spans * rows * cols * stored, 2 * tiles.size + spans * 4 * rows * stored
        ),
        name="static_parts",
    )(slots, tiles, hist_slices, replaced)


def fill_left(left, gath_ref, section, halves, parts, width):
    for half in range(halves):
        for part in range(parts):
            first = (half * parts + part) * width
            place = lax.rem(section - part + parts, parts)
            left[:, first : first + width] = gath_ref[half, place]


def layer_step(place, gathered, support, slices, static, columns, layer, beta, row_devices):
    halves, parts, picks, width = gathered.shape
    spans, rows, _ = static.shape
    rows_local = rows // row_devices
    depth = halves * parts * width
    step = ROW_CHUNK // rows_local
    chunks = row_devices // step

    def kernel(place_ref, gath_ref, sup_ref, static_ref, *refs):
        slice_refs, column_refs = refs[:parts], refs[parts : parts + spans]
        out_ref, left, left_sems, sup, sup_sem, right, right_sem, stat, stat_sems, cols_sems, sums, out_sems = refs[parts + spans : -spans]
        cols = refs[-spans:]
        section = place_ref[0]
        apart = lax.rem(section - layer + parts, parts)
        incoming = []
        for half in range(halves):
            for part in range(parts):
                first = (half * parts + part) * width
                incoming.append(
                    pltpu.make_async_copy(
                        gath_ref.at[half, lax.rem(section - part + parts, parts)],
                        left.at[:, first : first + width],
                        left_sems.at[half, part],
                    )
                )
        incoming.append(pltpu.make_async_copy(sup_ref, sup, sup_sem))
        for copy in incoming:
            copy.start()
        for by in range(parts):
            @pl.when(apart == by)
            def _():
                pltpu.make_async_copy(slice_refs[by], right, right_sem).start()

        later = []
        for span in range(spans):
            pair = (
                pltpu.make_async_copy(column_refs[span], cols[span], cols_sems.at[span]),
                pltpu.make_async_copy(static_ref.at[span], stat.at[span], stat_sems.at[span]),
            )
            for copy in pair:
                copy.start()
            later.append(pair)
        for copy in incoming:
            copy.wait()
        pltpu.make_async_copy(slice_refs[0], right, right_sem).wait()
        projected = jnp.dot(left[...], right[...], preferred_element_type=jnp.float32)
        fresh = jnp.maximum(
            (1.0 - beta) * sup[...].astype(jnp.float32) + beta * projected, 0.0
        ).astype(jnp.bfloat16)
        outgoing = []
        for span in range(spans):
            used = (span + 1) * rows_local
            for copy in later[span]:
                copy.wait()
            for chunk in range(chunks):
                first = chunk * step
                at = slice(chunk * ROW_CHUNK, (chunk + 1) * ROW_CHUNK)
                part = stat[span, at] + jnp.dot(
                    cols[span][at], fresh[:used], preferred_element_type=jnp.float32
                )
                sums[span, first : first + step] = part.astype(jnp.bfloat16).reshape(
                    step, rows_local, width
                )
                outgoing.append(
                    pltpu.make_async_copy(
                        sums.at[span, first : first + step],
                        out_ref.at[first : first + step, span],
                        out_sems.at[span, chunk],
                    )
                )
                outgoing[-1].start()
        for copy in outgoing:
            copy.wait()

    return pl.pallas_call(
        kernel,
        out_shape=jax.ShapeDtypeStruct((row_devices, spans, rows_local, width), jnp.bfloat16),
        in_specs=[IN_SMEM] + [IN_HBM] * (3 + parts + spans),
        out_specs=IN_HBM,
        scratch_shapes=[
            pltpu.VMEM((picks, depth), jnp.bfloat16),
            pltpu.SemaphoreType.DMA((halves, parts)),
            pltpu.VMEM((picks, width), jnp.bfloat16),
            pltpu.SemaphoreType.DMA(()),
            pltpu.VMEM((depth, width), jnp.bfloat16),
            pltpu.SemaphoreType.DMA(()),
            pltpu.VMEM(static.shape, jnp.float32),
            pltpu.SemaphoreType.DMA((spans,)),
            pltpu.SemaphoreType.DMA((spans,)),
            pltpu.VMEM((spans, row_devices, rows_local, width), jnp.bfloat16),
            pltpu.SemaphoreType.DMA((spans, chunks)),
            *[pltpu.VMEM(each.shape, jnp.bfloat16) for each in columns],
        ],
        compiler_params=vmem_params(KERNEL_VMEM),
        cost_estimate=cost(
            2 * picks * depth * width + 2 * spans * rows * width * picks,
            6 * spans * rows * width + 2 * spans * rows * picks,
        ),
        name="layer_step",
    )(place, gathered, support, static, *slices, *columns)


def whole_rows(place, betas, gathered, weight_cols, earlier, layer):
    halves, parts, picks, width = gathered.shape
    depth, half = weight_cols.shape

    def kernel(place_ref, betas_ref, gath_ref, w_ref, *refs):
        if layer:
            earlier_ref, out_ref, left, own = refs
        else:
            out_ref, left, own = refs
        section, feat = place_ref[0], place_ref[1]

        @pl.when(section == layer)
        def _():
            beta = betas_ref[layer]
            fill_left(left, gath_ref, section, halves, parts, width)
            for part in range(parts):
                own[:, part * width : (part + 1) * width] = gath_ref[
                    feat, lax.rem(section - part + parts, parts)
                ]
            projected = jnp.dot(left[...], w_ref[...], preferred_element_type=jnp.float32)
            out_ref[...] = jnp.maximum(
                (1.0 - beta) * own[...].astype(jnp.float32) + beta * projected, 0.0
            ).astype(jnp.bfloat16)

        @pl.when(section != layer)
        def _():
            out_ref[...] = earlier_ref[...] if layer else jnp.zeros_like(out_ref)

    operands = [gathered, weight_cols] + ([earlier] if layer else [])
    return pl.pallas_call(
        kernel,
        out_shape=jax.ShapeDtypeStruct((picks, half), jnp.bfloat16),
        in_specs=[pl.BlockSpec(memory_space=pltpu.SMEM)] * 2
        + [pl.BlockSpec(memory_space=pltpu.VMEM)] * len(operands),
        scratch_shapes=[
            pltpu.VMEM((picks, depth), jnp.bfloat16),
            pltpu.VMEM((picks, half), jnp.bfloat16),
        ],
        compiler_params=vmem_params(16),
        cost_estimate=cost(2 * picks * depth * half, 2 * (picks * depth + depth * half)),
        name="whole_rows",
    )(place, betas, *operands)


def replace_rows(stored, ids, fresh):
    owned, half = stored.shape
    picks = ids.shape[1]
    chunk = 512

    def kernel(stored_ref, ids_ref, fresh_ref, out_ref):
        first = pl.program_id(0) * chunk
        vertex = first + lax.broadcasted_iota(jnp.int32, (chunk, picks), 0)
        hits = (vertex == ids_ref[...]).astype(jnp.float32)
        placed = jnp.dot(
            hits.astype(jnp.bfloat16), fresh_ref[...], preferred_element_type=jnp.float32
        )
        found = jnp.sum(hits, axis=1, keepdims=True) > 0
        out_ref[...] = jnp.where(found, placed, stored_ref[...].astype(jnp.float32)).astype(
            jnp.bfloat16
        )

    return pl.pallas_call(
        kernel,
        out_shape=jax.ShapeDtypeStruct((owned, half), jnp.bfloat16),
        grid=(owned // chunk,),
        in_specs=[
            pl.BlockSpec((chunk, half), lambda i: (i, 0)),
            pl.BlockSpec((1, picks), lambda i: (0, 0)),
            pl.BlockSpec((picks, half), lambda i: (0, 0)),
        ],
        out_specs=pl.BlockSpec((chunk, half), lambda i: (i, 0)),
        compiler_params=vmem_params(24),
        cost_estimate=cost(2 * owned * picks * half, 4 * owned * half),
        name="replace_rows",
    )(stored, ids, fresh)


def shards(features, history, weights, tile_values, tile_rows, tile_cols, tile_counts, span_ids):
    spans, rows_local = span_ids.shape
    side = tile_values.shape[2]
    owned, half = features.shape
    layers = lax.axis_size("section")
    row_devices = lax.axis_size("vertex")
    section = lax.axis_index("section")
    width = half // layers
    picks = spans * rows_local
    depth = weights.shape[1]
    betas = [math.log(BETA_SCALE / (layer + 1) + 1.0) for layer in range(layers)]
    place = jnp.stack([section, lax.axis_index("feat")]).astype(jnp.int32)
    beta_table = jnp.array(betas, jnp.float32)

    stored = history[0]
    hist_slices = lax.all_to_all(section_slices(stored, layers), "section", 0, 0, tiled=True)

    select, replaced = selection(span_ids, owned, width)
    ids = span_ids.reshape(1, picks)
    feat_slice = lax.dynamic_slice_in_dim(features, section * width, width, 1)
    initial_half = jnp.take(features, ids[0], axis=0)
    initial = lax.dynamic_slice_in_dim(initial_half, section * width, width, 1).astype(jnp.float32)
    col_blocks = owned // side
    blocks = rows_local * row_devices // side * col_blocks
    slot_count = tile_rows.shape[1]
    listed = jnp.arange(slot_count)[None, :]
    key = jnp.where(listed < tile_counts, tile_rows * col_blocks + tile_cols, blocks)
    here = key[:, :, None] == jnp.arange(blocks)[None, None, :]
    slots = slot_count + jnp.sum(
        jnp.where(here, listed[:, :, None] - slot_count, 0), axis=1, dtype=jnp.int32
    )
    columns = replaced_columns(tile_values, slots, select)
    hist_slices, replaced, feat_slice, initial, slots, columns = lax.optimization_barrier(
        (hist_slices, replaced, feat_slice, initial, slots, columns)
    )
    partial, static_one = first_partial(
        tile_values, slots, hist_slices, feat_slice, replaced, row_devices
    )
    own_weights = after(weights[0], partial)
    statics = [static_one, *static_parts(tile_values, slots, after(hist_slices, partial), replaced)]
    by_distance = [
        lax.dynamic_slice_in_dim(own_weights, (section + by) % layers * width, width, 1)
        for by in range(layers)
    ]
    weight_slices = [by_distance[0]] + [
        rotated(by_distance[by], "section", by) for by in range(1, layers)
    ]

    rows_kept = table = None
    for layer in range(layers):
        if layer == layers - 1:
            before = rotated(rows_kept, "section", 1)
            table = replace_rows(stored, ids, jnp.where(section == 0, initial_half, before))
        arrived = lax.all_to_all(partial, "vertex", 0, 0, tiled=True)
        if layer == 0:
            arrived, statics, weight_slices = lax.optimization_barrier(
                (arrived, statics, weight_slices)
            )
        if table is not None:
            arrived, table = lax.optimization_barrier((arrived, table))
        support = collect(arrived, initial)
        near = jnp.stack([support] + [rotated(support, "section", by) for by in range(1, layers)])
        gathered = lax.all_gather(near, "feat", axis=0)
        if layer < layers - 1:
            partial = layer_step(
                place,
                gathered,
                support,
                weight_slices,
                statics[layer],
                columns,
                layer,
                betas[layer],
                row_devices,
            )
        rows_kept = whole_rows(place, beta_table, gathered, own_weights, rows_kept, layer)
    return (rows_kept.reshape(1, spans, rows_local, half), table[None])


def solution(mesh):
    placed = (
        P("vertex", "feat"),
        P("section", "vertex", "feat"),
        P("section", None, "feat"),
        P(None, "vertex", None, None),
        P(None, "vertex"),
        P(None, "vertex"),
        P(None, "vertex"),
        P(None, "vertex"),
    )
    return jax.shard_map(
        shards,
        mesh=mesh,
        in_specs=placed,
        out_specs=(P("section", None, "vertex", "feat"), P("section", "vertex", "feat")),
        check_vma=False,
    )
```

```python
import math

import jax
import jax.numpy as jnp
from jax import lax
from jax.experimental import pallas as pl
from jax.experimental.pallas import tpu as pltpu
from jax.sharding import PartitionSpec as P

RESIDUAL_SHARE = 0.2
BETA_SCALE = 0.5
MIB = 1 << 20
ROW_CHUNK = 1024
KERNEL_VMEM = 58
IN_HBM = pl.BlockSpec(memory_space=pltpu.HBM)
IN_VMEM = pl.BlockSpec(memory_space=pltpu.VMEM)
IN_SMEM = pl.BlockSpec(memory_space=pltpu.SMEM)


def rotated(array, axis, by):
    devices = lax.axis_size(axis)
    return lax.ppermute(array, axis, [(i, (i + by) % devices) for i in range(devices)])


def after(array, earlier):
    return lax.optimization_barrier((array, earlier))[0]


def vmem_params(mib):
    return pltpu.CompilerParams(vmem_limit_bytes=mib * MIB)


def cost(flops, bytes_accessed):
    return pl.CostEstimate(flops=flops, transcendentals=0, bytes_accessed=bytes_accessed)


def rows_from(tiles_ref, slots_ref, span, first, count, col_blocks):
    lines = []
    for row in range(count):
        base = (first + row) * col_blocks
        lines.append(
            jnp.concatenate(
                [tiles_ref[span, slots_ref[span, base + col]] for col in range(col_blocks)], axis=1
            )
        )
    return jnp.concatenate(lines, axis=0)


def multiply(tiles_ref, slots_ref, span, right, width, put, unrolled=False):
    side = tiles_ref.shape[-1]
    col_blocks = right.shape[0] // side
    row_blocks = slots_ref.shape[1] // col_blocks
    step = ROW_CHUNK // side

    def chunk(first):
        left = rows_from(tiles_ref, slots_ref, span, first, step, col_blocks)
        part = jnp.dot(left, right[:, :width], preferred_element_type=jnp.float32)
        put(pl.ds(pl.multiple_of(first * side, side), ROW_CHUNK), part)

    if unrolled:
        for first in range(0, row_blocks, step):
            chunk(first)
    else:
        pl.loop(0, row_blocks, step=step)(chunk)


def tile_copies(tiles_ref, held, sems):
    spans, slots = tiles_ref.shape[:2]
    return [
        pltpu.make_async_copy(
            tiles_ref.at[span], held.at[span, pl.ds(0, slots)], sems.at[span]
        )
        for span in range(spans)
    ]


def tile_scratch(tiles):
    spans, slots, side, _ = tiles.shape
    return [pltpu.VMEM((spans, slots + 1, side, side), jnp.bfloat16), pltpu.SemaphoreType.DMA((spans,))]


def first_partial(tiles, slots, hist_slices, feats, replaced, row_devices):
    spans, slot_count, side, _ = tiles.shape
    _, cols, width = hist_slices.shape
    col_blocks = cols // side
    row_blocks = slots.shape[1] // col_blocks

    def kernel(slots_ref, tiles_ref, hist_ref, feat_ref, mask_ref, out_ref, static_ref, held, tile_sems, hist, hist_sem, table, sums, out_sems, static, static_sems):
        hist_copy = pltpu.make_async_copy(hist_ref.at[pl.ds(0, 2)], hist, hist_sem)
        copies = tile_copies(tiles_ref, held, tile_sems)
        for copy in [hist_copy] + copies:
            copy.start()
        hist_copy.wait()
        outgoing = []
        for span in range(spans):
            held[span, slot_count] = jnp.zeros((side, side), jnp.bfloat16)
            replaces = mask_ref[span] > 0
            table[:, :width] = jnp.where(replaces, feat_ref[...], hist[0])
            table[:, width:] = jnp.where(replaces, jnp.zeros_like(hist[1]), hist[1])
            copies[span].wait()

            def put(at, part, span=span):
                sums[span, at] = part[:, :width].astype(jnp.bfloat16)
                static[span, at] = part[:, width:]

            multiply(held, slots_ref, span, table, 2 * width, put, unrolled=True)
            outgoing.append(
                pltpu.make_async_copy(static.at[span], static_ref.at[span], static_sems.at[span])
            )
            outgoing[-1].start()
            for device in range(row_devices):
                outgoing.append(
                    pltpu.make_async_copy(
                        sums.at[span, pl.ds(device * side, side)],
                        out_ref.at[device, span],
                        out_sems.at[span, device],
                    )
                )
                outgoing[-1].start()
        for copy in outgoing:
            copy.wait()

    return pl.pallas_call(
        kernel,
        out_shape=(
            jax.ShapeDtypeStruct((row_devices, spans, side, width), jnp.bfloat16),
            jax.ShapeDtypeStruct((spans, row_blocks * side, width), jnp.float32),
        ),
        in_specs=[IN_SMEM, IN_HBM, IN_HBM, IN_VMEM, IN_VMEM],
        out_specs=(IN_HBM, IN_HBM),
        scratch_shapes=[
            *tile_scratch(tiles),
            pltpu.VMEM((2, cols, width), jnp.bfloat16),
            pltpu.SemaphoreType.DMA(()),
            pltpu.VMEM((cols, 2 * width), jnp.bfloat16),
            pltpu.VMEM((spans, row_blocks * side, width), jnp.bfloat16),
            pltpu.SemaphoreType.DMA((spans, row_devices)),
            pltpu.VMEM((spans, row_blocks * side, width), jnp.float32),
            pltpu.SemaphoreType.DMA((spans,)),
        ],
        compiler_params=vmem_params(KERNEL_VMEM),
        cost_estimate=cost(4 * spans * row_blocks * side * cols * width, 2 * tiles.size),
        name="first_partial",
    )(slots, tiles, hist_slices, feats, replaced)


def section_slices(array, parts):
    rows, cols = array.shape
    width = cols // parts
    groups = 2
    each = rows // groups

    def kernel(in_ref, out_ref, held, in_sems, out_sems):
        moves = []
        for group in range(groups):
            at = pl.ds(group * each, each)
            for part in range(parts):
                moves.append(
                    (
                        pltpu.make_async_copy(
                            in_ref.at[at, pl.ds(part * width, width)],
                            held.at[part, at],
                            in_sems.at[part, group],
                        ),
                        pltpu.make_async_copy(
                            held.at[part, at], out_ref.at[part, at], out_sems.at[part, group]
                        ),
                    )
                )
        for first, _ in moves:
            first.start()
        for first, second in moves:
            first.wait()
            second.start()
        for _, second in moves:
            second.wait()

    return pl.pallas_call(
        kernel,
        out_shape=jax.ShapeDtypeStruct((parts, rows, width), array.dtype),
        in_specs=[IN_HBM],
        out_specs=IN_HBM,
        scratch_shapes=[
            pltpu.VMEM((parts, rows, width), array.dtype),
            pltpu.SemaphoreType.DMA((parts, groups)),
            pltpu.SemaphoreType.DMA((parts, groups)),
        ],
        compiler_params=vmem_params(KERNEL_VMEM),
        cost_estimate=cost(0, 4 * rows * cols),
        name="section_slices",
    )(array)


def selection(ids, owned, width):
    spans, rows_local = ids.shape
    picks = spans * rows_local
    chunk = 512

    def kernel(ids_ref, select_ref, mask_ref):
        first = pl.program_id(0) * chunk
        vertex = first + lax.broadcasted_iota(jnp.int32, (chunk, picks), 0)
        hits = (vertex == ids_ref[...]).astype(jnp.float32)
        select_ref[...] = hits.astype(jnp.bfloat16)
        total = jnp.zeros((chunk, 1), jnp.float32)
        for span in range(spans):
            part = hits[:, span * rows_local : (span + 1) * rows_local]
            total = total + jnp.sum(part, axis=1, keepdims=True)
            mask_ref[span] = jnp.broadcast_to(total, (chunk, width)).astype(jnp.bfloat16)

    return pl.pallas_call(
        kernel,
        out_shape=(
            jax.ShapeDtypeStruct((owned, picks), jnp.bfloat16),
            jax.ShapeDtypeStruct((spans, owned, width), jnp.bfloat16),
        ),
        grid=(owned // chunk,),
        in_specs=[pl.BlockSpec((1, picks), lambda i: (0, 0))],
        out_specs=(
            pl.BlockSpec((chunk, picks), lambda i: (i, 0)),
            pl.BlockSpec((spans, chunk, width), lambda i: (0, i, 0)),
        ),
        compiler_params=vmem_params(16),
        cost_estimate=cost(owned * picks, 4 * owned * picks),
        name="selection",
    )(ids.reshape(1, picks))


def collect(arrived, initial):
    owners, spans, rows_local, width = arrived.shape

    groups = 4
    each = owners // groups

    def kernel(in_ref, init_ref, out_ref, held, sems, sums):
        copies = [
            pltpu.make_async_copy(
                in_ref.at[pl.ds(group * each, each)], held.at[pl.ds(group * each, each)], sems.at[group]
            )
            for group in range(groups)
        ]
        for copy in copies:
            copy.start()
        for group in range(groups):
            copies[group].wait()
            for span in range(spans):
                at = slice(span * rows_local, (span + 1) * rows_local)
                total = held[group * each, span].astype(jnp.float32)
                for owner in range(group * each + 1, (group + 1) * each):
                    total = total + held[owner, span].astype(jnp.float32)
                if group:
                    total = sums[at] + total
                if group < groups - 1:
                    sums[at] = total
                else:
                    out_ref[at] = (
                        (1.0 - RESIDUAL_SHARE) * total + RESIDUAL_SHARE * init_ref[at]
                    ).astype(jnp.bfloat16)

    return pl.pallas_call(
        kernel,
        out_shape=jax.ShapeDtypeStruct((spans * rows_local, width), jnp.bfloat16),
        in_specs=[IN_HBM, IN_VMEM],
        out_specs=IN_VMEM,
        scratch_shapes=[
            pltpu.VMEM(arrived.shape, jnp.bfloat16),
            pltpu.SemaphoreType.DMA((groups,)),
            pltpu.VMEM((spans * rows_local, width), jnp.float32),
        ],
        compiler_params=vmem_params(16),
        cost_estimate=cost(arrived.size, 2 * arrived.size),
        name="collect",
    )(arrived, initial)


def replaced_columns(tiles, slots, select):
    spans, slot_count, side, _ = tiles.shape
    cols, picks = select.shape
    rows = slots.shape[1] // (cols // side) * side
    rows_local = picks // spans

    def kernel(slots_ref, tiles_ref, sel_ref, *refs):
        column_refs, (held, tile_sems, sends) = refs[:spans], refs[spans : spans + 3]
        kept = refs[spans + 3 :]
        copies = tile_copies(tiles_ref, held, tile_sems)
        for copy in copies:
            copy.start()
        outgoing = []
        for span in range(spans):
            used = (span + 1) * rows_local
            held[span, slot_count] = jnp.zeros((side, side), jnp.bfloat16)
            copies[span].wait()

            def put(at, part, span=span):
                kept[span][at] = part.astype(jnp.bfloat16)

            multiply(held, slots_ref, span, sel_ref, used, put)
            outgoing.append(pltpu.make_async_copy(kept[span], column_refs[span], sends.at[span]))
            outgoing[-1].start()
        for copy in outgoing:
            copy.wait()

    shapes = [(rows, (span + 1) * rows_local) for span in range(spans)]
    return pl.pallas_call(
        kernel,
        out_shape=tuple(jax.ShapeDtypeStruct(shape, jnp.bfloat16) for shape in shapes),
        in_specs=[IN_SMEM, IN_HBM, IN_VMEM],
        out_specs=(IN_HBM,) * spans,
        scratch_shapes=[
            *tile_scratch(tiles),
            pltpu.SemaphoreType.DMA((spans,)),
            *[pltpu.VMEM(shape, jnp.bfloat16) for shape in shapes],
        ],
        compiler_params=vmem_params(KERNEL_VMEM),
        cost_estimate=cost(2 * spans * rows * cols * picks, 2 * tiles.size + 6 * rows * picks),
        name="replaced_columns",
    )(slots, tiles, select)


def static_parts(tiles, slots, hist_slices, replaced):
    spans, slot_count, side, _ = tiles.shape
    layers, cols, width = hist_slices.shape
    rows = slots.shape[1] // (cols // side) * side
    kinds = layers - 2
    stored = kinds * width

    def kernel(slots_ref, tiles_ref, hist_ref, mask_ref, *refs):
        static_refs = refs[:kinds]
        held, tile_sems, hist, hist_sem, right, sums, sends = refs[kinds:]
        hist_copy = pltpu.make_async_copy(hist_ref.at[pl.ds(2, kinds)], hist, hist_sem)
        copies = tile_copies(tiles_ref, held, tile_sems)
        for copy in [hist_copy] + copies:
            copy.start()
        hist_copy.wait()
        outgoing = []
        for span in range(spans):
            held[span, slot_count] = jnp.zeros((side, side), jnp.bfloat16)
            for index in range(kinds):
                right[:, index * width : (index + 1) * width] = jnp.where(
                    mask_ref[span] > 0, jnp.zeros_like(hist[index]), hist[index]
                )
            copies[span].wait()

            def put(at, part, span=span):
                for index in range(kinds):
                    sums[index, span, at] = part[:, index * width : (index + 1) * width]

            multiply(held, slots_ref, span, right, stored, put)
            for index in range(kinds):
                outgoing.append(
                    pltpu.make_async_copy(
                        sums.at[index, span], static_refs[index].at[span], sends.at[index, span]
                    )
                )
                outgoing[-1].start()
        for copy in outgoing:
            copy.wait()

    return pl.pallas_call(
        kernel,
        out_shape=(jax.ShapeDtypeStruct((spans, rows, width), jnp.float32),) * kinds,
        in_specs=[IN_SMEM, IN_HBM, IN_HBM, IN_VMEM],
        out_specs=(IN_HBM,) * kinds,
        scratch_shapes=[
            *tile_scratch(tiles),
            pltpu.VMEM((kinds, cols, width), jnp.bfloat16),
            pltpu.SemaphoreType.DMA(()),
            pltpu.VMEM((cols, stored), jnp.bfloat16),
            pltpu.VMEM((kinds, spans, rows, width), jnp.float32),
            pltpu.SemaphoreType.DMA((kinds, spans)),
        ],
        compiler_params=vmem_params(KERNEL_VMEM),
        cost_estimate=cost(
            2 * spans * rows * cols * stored, 2 * tiles.size + spans * 4 * rows * stored
        ),
        name="static_parts",
    )(slots, tiles, hist_slices, replaced)


def fill_left(left, gath_ref, section, halves, parts, width):
    for half in range(halves):
        for part in range(parts):
            first = (half * parts + part) * width
            place = lax.rem(section - part + parts, parts)
            left[:, first : first + width] = gath_ref[half, place]


def layer_step(place, gathered, support, slices, static, columns, layer, beta, row_devices, resident):
    halves, parts, picks, width = gathered.shape
    spans, rows, _ = static.shape
    rows_local = rows // row_devices
    depth = halves * parts * width
    step = ROW_CHUNK // rows_local
    chunks = row_devices // step

    heavy = IN_VMEM if resident else IN_HBM
    small = (1, 16, 128)

    def kernel(place_ref, gath_ref, sup_ref, static_ref, *refs):
        slice_refs, column_refs = refs[:parts], refs[parts : parts + spans]
        out_ref, left, left_sems, sup, sup_sem, right, right_sem, stat, stat_sems, cols_sems, sums, out_sems = refs[parts + spans : -spans]
        cols = refs[-spans:]
        section = place_ref[0]
        apart = lax.rem(section - layer + parts, parts)
        incoming = []
        for half in range(halves):
            for part in range(parts):
                first = (half * parts + part) * width
                incoming.append(
                    pltpu.make_async_copy(
                        gath_ref.at[half, lax.rem(section - part + parts, parts)],
                        left.at[:, first : first + width],
                        left_sems.at[half, part],
                    )
                )
        incoming.append(pltpu.make_async_copy(sup_ref, sup, sup_sem))
        for copy in incoming:
            copy.start()
        for by in range(parts):
            @pl.when(apart == by)
            def _():
                pltpu.make_async_copy(slice_refs[by], right, right_sem).start()

        later = [()] * spans
        if resident:
            cols, stat = column_refs, static_ref
        else:
            for span in range(spans):
                later[span] = (
                    pltpu.make_async_copy(column_refs[span], cols[span], cols_sems.at[span]),
                    pltpu.make_async_copy(static_ref.at[span], stat.at[span], stat_sems.at[span]),
                )
                for copy in later[span]:
                    copy.start()

        for copy in incoming:
            copy.wait()
        pltpu.make_async_copy(slice_refs[0], right, right_sem).wait()
        projected = jnp.dot(left[...], right[...], preferred_element_type=jnp.float32)
        fresh = jnp.maximum(
            (1.0 - beta) * sup[...].astype(jnp.float32) + beta * projected, 0.0
        ).astype(jnp.bfloat16)
        outgoing = []
        for span in range(spans):
            used = (span + 1) * rows_local
            for copy in later[span]:
                copy.wait()
            for chunk in range(chunks):
                first = chunk * step
                at = slice(chunk * ROW_CHUNK, (chunk + 1) * ROW_CHUNK)
                part = stat[span, at] + jnp.dot(
                    cols[span][at], fresh[:used], preferred_element_type=jnp.float32
                )
                sums[span, first : first + step] = part.astype(jnp.bfloat16).reshape(
                    step, rows_local, width
                )
                outgoing.append(
                    pltpu.make_async_copy(
                        sums.at[span, first : first + step],
                        out_ref.at[first : first + step, span],
                        out_sems.at[span, chunk],
                    )
                )
                outgoing[-1].start()
        for copy in outgoing:
            copy.wait()

    return pl.pallas_call(
        kernel,
        out_shape=jax.ShapeDtypeStruct((row_devices, spans, rows_local, width), jnp.bfloat16),
        in_specs=[IN_SMEM, IN_HBM, IN_HBM, heavy] + [IN_HBM] * parts + [heavy] * spans,
        out_specs=IN_HBM,
        scratch_shapes=[
            pltpu.VMEM((picks, depth), jnp.bfloat16),
            pltpu.SemaphoreType.DMA((halves, parts)),
            pltpu.VMEM((picks, width), jnp.bfloat16),
            pltpu.SemaphoreType.DMA(()),
            pltpu.VMEM((depth, width), jnp.bfloat16),
            pltpu.SemaphoreType.DMA(()),
            pltpu.VMEM(small if resident else static.shape, jnp.float32),
            pltpu.SemaphoreType.DMA((spans,)),
            pltpu.SemaphoreType.DMA((spans,)),
            pltpu.VMEM((spans, row_devices, rows_local, width), jnp.bfloat16),
            pltpu.SemaphoreType.DMA((spans, chunks)),
            *[pltpu.VMEM(small if resident else each.shape, jnp.bfloat16) for each in columns],
        ],
        compiler_params=vmem_params(16 if resident else KERNEL_VMEM),
        cost_estimate=cost(
            2 * picks * depth * width + 2 * spans * rows * width * picks,
            6 * spans * rows * width + 2 * spans * rows * picks,
        ),
        name="layer_step",
    )(place, gathered, support, static, *slices, *columns)


def whole_rows(place, betas, gathered, weight_cols, earlier, layer):
    halves, parts, picks, width = gathered.shape
    depth, half = weight_cols.shape

    def kernel(place_ref, betas_ref, gath_ref, w_ref, *refs):
        if layer:
            earlier_ref, out_ref, left, own = refs
        else:
            out_ref, left, own = refs
        section, feat = place_ref[0], place_ref[1]

        @pl.when(section == layer)
        def _():
            beta = betas_ref[layer]
            fill_left(left, gath_ref, section, halves, parts, width)
            for part in range(parts):
                own[:, part * width : (part + 1) * width] = gath_ref[
                    feat, lax.rem(section - part + parts, parts)
                ]
            projected = jnp.dot(left[...], w_ref[...], preferred_element_type=jnp.float32)
            out_ref[...] = jnp.maximum(
                (1.0 - beta) * own[...].astype(jnp.float32) + beta * projected, 0.0
            ).astype(jnp.bfloat16)

        @pl.when(section != layer)
        def _():
            out_ref[...] = earlier_ref[...] if layer else jnp.zeros_like(out_ref)

    operands = [gathered, weight_cols] + ([earlier] if layer else [])
    return pl.pallas_call(
        kernel,
        out_shape=jax.ShapeDtypeStruct((picks, half), jnp.bfloat16),
        in_specs=[pl.BlockSpec(memory_space=pltpu.SMEM)] * 2
        + [pl.BlockSpec(memory_space=pltpu.VMEM)] * len(operands),
        scratch_shapes=[
            pltpu.VMEM((picks, depth), jnp.bfloat16),
            pltpu.VMEM((picks, half), jnp.bfloat16),
        ],
        compiler_params=vmem_params(16),
        cost_estimate=cost(2 * picks * depth * half, 2 * (picks * depth + depth * half)),
        name="whole_rows",
    )(place, betas, *operands)


def replace_rows(stored, ids, fresh):
    owned, half = stored.shape
    picks = ids.shape[1]
    chunk = 512

    def kernel(stored_ref, ids_ref, fresh_ref, out_ref):
        first = pl.program_id(0) * chunk
        vertex = first + lax.broadcasted_iota(jnp.int32, (chunk, picks), 0)
        hits = (vertex == ids_ref[...]).astype(jnp.float32)
        placed = jnp.dot(
            hits.astype(jnp.bfloat16), fresh_ref[...], preferred_element_type=jnp.float32
        )
        found = jnp.sum(hits, axis=1, keepdims=True) > 0
        out_ref[...] = jnp.where(found, placed, stored_ref[...].astype(jnp.float32)).astype(
            jnp.bfloat16
        )

    return pl.pallas_call(
        kernel,
        out_shape=jax.ShapeDtypeStruct((owned, half), jnp.bfloat16),
        grid=(owned // chunk,),
        in_specs=[
            pl.BlockSpec((chunk, half), lambda i: (i, 0)),
            pl.BlockSpec((1, picks), lambda i: (0, 0)),
            pl.BlockSpec((picks, half), lambda i: (0, 0)),
        ],
        out_specs=pl.BlockSpec((chunk, half), lambda i: (i, 0)),
        compiler_params=vmem_params(24),
        cost_estimate=cost(2 * owned * picks * half, 4 * owned * half),
        name="replace_rows",
    )(stored, ids, fresh)


def shards(features, history, weights, tile_values, tile_rows, tile_cols, tile_counts, span_ids):
    spans, rows_local = span_ids.shape
    side = tile_values.shape[2]
    owned, half = features.shape
    layers = lax.axis_size("section")
    row_devices = lax.axis_size("vertex")
    section = lax.axis_index("section")
    width = half // layers
    picks = spans * rows_local
    depth = weights.shape[1]
    betas = [math.log(BETA_SCALE / (layer + 1) + 1.0) for layer in range(layers)]
    place = jnp.stack([section, lax.axis_index("feat")]).astype(jnp.int32)
    beta_table = jnp.array(betas, jnp.float32)

    stored = history[0]
    hist_slices = lax.all_to_all(section_slices(stored, layers), "section", 0, 0, tiled=True)

    select, replaced = selection(span_ids, owned, width)
    ids = span_ids.reshape(1, picks)
    feat_slice = lax.dynamic_slice_in_dim(features, section * width, width, 1)
    initial_half = jnp.take(features, ids[0], axis=0)
    initial = lax.dynamic_slice_in_dim(initial_half, section * width, width, 1).astype(jnp.float32)
    col_blocks = owned // side
    blocks = rows_local * row_devices // side * col_blocks
    slot_count = tile_rows.shape[1]
    listed = jnp.arange(slot_count)[None, :]
    key = jnp.where(listed < tile_counts, tile_rows * col_blocks + tile_cols, blocks)
    here = key[:, :, None] == jnp.arange(blocks)[None, None, :]
    slots = slot_count + jnp.sum(
        jnp.where(here, listed[:, :, None] - slot_count, 0), axis=1, dtype=jnp.int32
    )
    columns = replaced_columns(tile_values, slots, select)
    hist_slices, replaced, feat_slice, initial, slots, columns = lax.optimization_barrier(
        (hist_slices, replaced, feat_slice, initial, slots, columns)
    )
    partial, static_one = first_partial(
        tile_values, slots, hist_slices, feat_slice, replaced, row_devices
    )
    own_weights = after(weights[0], partial)
    statics = [static_one, *static_parts(tile_values, slots, after(hist_slices, partial), replaced)]
    by_distance = [
        lax.dynamic_slice_in_dim(own_weights, (section + by) % layers * width, width, 1)
        for by in range(layers)
    ]
    weight_slices = [by_distance[0]] + [
        rotated(by_distance[by], "section", by) for by in range(1, layers)
    ]

    rows_kept = table = None
    for layer in range(layers):
        if layer == layers - 1:
            before = rotated(rows_kept, "section", 1)
            table = replace_rows(stored, ids, jnp.where(section == 0, initial_half, before))
        arrived = lax.all_to_all(partial, "vertex", 0, 0, tiled=True)
        if layer == 0:
            arrived, statics, weight_slices = lax.optimization_barrier(
                (arrived, statics, weight_slices)
            )
        if table is not None:
            arrived, table = lax.optimization_barrier((arrived, table))
        support = collect(arrived, initial)
        near = jnp.stack([support] + [rotated(support, "section", by) for by in range(1, layers)])
        gathered = lax.all_gather(near, "feat", axis=0)
        if layer < layers - 1:
            partial = layer_step(
                place,
                gathered,
                support,
                weight_slices,
                statics[layer],
                columns,
                layer,
                betas[layer],
                row_devices,
                layer > 0,
            )
        rows_kept = whole_rows(place, beta_table, gathered, own_weights, rows_kept, layer)
    return (rows_kept.reshape(1, spans, rows_local, half), table[None])


def solution(mesh):
    placed = (
        P("vertex", "feat"),
        P("section", "vertex", "feat"),
        P("section", None, "feat"),
        P(None, "vertex", None, None),
        P(None, "vertex"),
        P(None, "vertex"),
        P(None, "vertex"),
        P(None, "vertex"),
    )
    return jax.shard_map(
        shards,
        mesh=mesh,
        in_specs=placed,
        out_specs=(P("section", None, "vertex", "feat"), P("section", "vertex", "feat")),
        check_vma=False,
    )
```

```python
import math

import jax
import jax.numpy as jnp
from jax import lax
from jax.experimental import pallas as pl
from jax.experimental.pallas import tpu as pltpu
from jax.sharding import PartitionSpec as P

RESIDUAL_SHARE = 0.2
BETA_SCALE = 0.5
MIB = 1 << 20
ROW_CHUNK = 1024
KERNEL_VMEM = 58
IN_HBM = pl.BlockSpec(memory_space=pltpu.HBM)
IN_VMEM = pl.BlockSpec(memory_space=pltpu.VMEM)
IN_SMEM = pl.BlockSpec(memory_space=pltpu.SMEM)


def rotated(array, axis, by):
    devices = lax.axis_size(axis)
    return lax.ppermute(array, axis, [(i, (i + by) % devices) for i in range(devices)])


def after(array, earlier):
    return lax.optimization_barrier((array, earlier))[0]


def vmem_params(mib):
    return pltpu.CompilerParams(vmem_limit_bytes=mib * MIB)


def cost(flops, bytes_accessed):
    return pl.CostEstimate(flops=flops, transcendentals=0, bytes_accessed=bytes_accessed)


def rows_from(tiles_ref, slots_ref, span, first, count, col_blocks):
    lines = []
    for row in range(count):
        base = (first + row) * col_blocks
        lines.append(
            jnp.concatenate(
                [tiles_ref[span, slots_ref[span, base + col]] for col in range(col_blocks)], axis=1
            )
        )
    return jnp.concatenate(lines, axis=0)


def multiply(tiles_ref, slots_ref, span, right, width, put, unrolled=False):
    side = tiles_ref.shape[-1]
    col_blocks = right.shape[0] // side
    row_blocks = slots_ref.shape[1] // col_blocks
    step = ROW_CHUNK // side

    def chunk(first):
        left = rows_from(tiles_ref, slots_ref, span, first, step, col_blocks)
        part = jnp.dot(left, right[:, :width], preferred_element_type=jnp.float32)
        put(pl.ds(pl.multiple_of(first * side, side), ROW_CHUNK), part)

    if unrolled:
        for first in range(0, row_blocks, step):
            chunk(first)
    else:
        pl.loop(0, row_blocks, step=step)(chunk)


def tile_copies(tiles_ref, held, sems):
    spans, slots = tiles_ref.shape[:2]
    return [
        pltpu.make_async_copy(
            tiles_ref.at[span], held.at[span, pl.ds(0, slots)], sems.at[span]
        )
        for span in range(spans)
    ]


def tile_scratch(tiles):
    spans, slots, side, _ = tiles.shape
    return [pltpu.VMEM((spans, slots + 1, side, side), jnp.bfloat16), pltpu.SemaphoreType.DMA((spans,))]


def first_partial(tiles, slots, hist_slices, feats, replaced, row_devices):
    spans, slot_count, side, _ = tiles.shape
    _, cols, width = hist_slices.shape
    col_blocks = cols // side
    row_blocks = slots.shape[1] // col_blocks

    def kernel(slots_ref, tiles_ref, hist_ref, feat_ref, mask_ref, out_ref, static_ref, held, tile_sems, hist, hist_sem, table, sums, out_sems, static, static_sems):
        hist_copy = pltpu.make_async_copy(hist_ref.at[pl.ds(0, 2)], hist, hist_sem)
        copies = tile_copies(tiles_ref, held, tile_sems)
        for copy in [hist_copy] + copies:
            copy.start()
        hist_copy.wait()
        outgoing = []
        for span in range(spans):
            held[span, slot_count] = jnp.zeros((side, side), jnp.bfloat16)
            replaces = mask_ref[span] > 0
            table[:, :width] = jnp.where(replaces, feat_ref[...], hist[0])
            table[:, width:] = jnp.where(replaces, jnp.zeros_like(hist[1]), hist[1])
            copies[span].wait()

            def put(at, part, span=span):
                sums[span, at] = part[:, :width].astype(jnp.bfloat16)
                static[span, at] = part[:, width:]

            multiply(held, slots_ref, span, table, 2 * width, put, unrolled=True)
            outgoing.append(
                pltpu.make_async_copy(static.at[span], static_ref.at[span], static_sems.at[span])
            )
            outgoing[-1].start()
            for device in range(row_devices):
                outgoing.append(
                    pltpu.make_async_copy(
                        sums.at[span, pl.ds(device * side, side)],
                        out_ref.at[device, span],
                        out_sems.at[span, device],
                    )
                )
                outgoing[-1].start()
        for copy in outgoing:
            copy.wait()

    return pl.pallas_call(
        kernel,
        out_shape=(
            jax.ShapeDtypeStruct((row_devices, spans, side, width), jnp.bfloat16),
            jax.ShapeDtypeStruct((spans, row_blocks * side, width), jnp.float32),
        ),
        in_specs=[IN_SMEM, IN_HBM, IN_HBM, IN_VMEM, IN_VMEM],
        out_specs=(IN_HBM, IN_HBM),
        scratch_shapes=[
            *tile_scratch(tiles),
            pltpu.VMEM((2, cols, width), jnp.bfloat16),
            pltpu.SemaphoreType.DMA(()),
            pltpu.VMEM((cols, 2 * width), jnp.bfloat16),
            pltpu.VMEM((spans, row_blocks * side, width), jnp.bfloat16),
            pltpu.SemaphoreType.DMA((spans, row_devices)),
            pltpu.VMEM((spans, row_blocks * side, width), jnp.float32),
            pltpu.SemaphoreType.DMA((spans,)),
        ],
        compiler_params=vmem_params(KERNEL_VMEM),
        cost_estimate=cost(4 * spans * row_blocks * side * cols * width, 2 * tiles.size),
        name="first_partial",
    )(slots, tiles, hist_slices, feats, replaced)


def section_slices(array, parts):
    rows, cols = array.shape
    width = cols // parts
    groups = 2
    each = rows // groups

    def kernel(in_ref, out_ref, held, in_sems, out_sems):
        moves = []
        for group in range(groups):
            at = pl.ds(group * each, each)
            for part in range(parts):
                moves.append(
                    (
                        pltpu.make_async_copy(
                            in_ref.at[at, pl.ds(part * width, width)],
                            held.at[part, at],
                            in_sems.at[part, group],
                        ),
                        pltpu.make_async_copy(
                            held.at[part, at], out_ref.at[part, at], out_sems.at[part, group]
                        ),
                    )
                )
        for first, _ in moves:
            first.start()
        for first, second in moves:
            first.wait()
            second.start()
        for _, second in moves:
            second.wait()

    return pl.pallas_call(
        kernel,
        out_shape=jax.ShapeDtypeStruct((parts, rows, width), array.dtype),
        in_specs=[IN_HBM],
        out_specs=IN_HBM,
        scratch_shapes=[
            pltpu.VMEM((parts, rows, width), array.dtype),
            pltpu.SemaphoreType.DMA((parts, groups)),
            pltpu.SemaphoreType.DMA((parts, groups)),
        ],
        compiler_params=vmem_params(KERNEL_VMEM),
        cost_estimate=cost(0, 4 * rows * cols),
        name="section_slices",
    )(array)


def selection(ids, owned, width):
    spans, rows_local = ids.shape
    picks = spans * rows_local
    chunk = 512

    def kernel(ids_ref, select_ref, mask_ref):
        first = pl.program_id(0) * chunk
        vertex = first + lax.broadcasted_iota(jnp.int32, (chunk, picks), 0)
        hits = (vertex == ids_ref[...]).astype(jnp.float32)
        select_ref[...] = hits.astype(jnp.bfloat16)
        total = jnp.zeros((chunk, 1), jnp.float32)
        for span in range(spans):
            part = hits[:, span * rows_local : (span + 1) * rows_local]
            total = total + jnp.sum(part, axis=1, keepdims=True)
            mask_ref[span] = jnp.broadcast_to(total, (chunk, width)).astype(jnp.bfloat16)

    return pl.pallas_call(
        kernel,
        out_shape=(
            jax.ShapeDtypeStruct((owned, picks), jnp.bfloat16),
            jax.ShapeDtypeStruct((spans, owned, width), jnp.bfloat16),
        ),
        grid=(owned // chunk,),
        in_specs=[pl.BlockSpec((1, picks), lambda i: (0, 0))],
        out_specs=(
            pl.BlockSpec((chunk, picks), lambda i: (i, 0)),
            pl.BlockSpec((spans, chunk, width), lambda i: (0, i, 0)),
        ),
        compiler_params=vmem_params(16),
        cost_estimate=cost(owned * picks, 4 * owned * picks),
        name="selection",
    )(ids.reshape(1, picks))


def collect(arrived, initial):
    owners, spans, rows_local, width = arrived.shape

    groups = 4
    each = owners // groups

    def kernel(in_ref, init_ref, out_ref, held, sems, sums):
        copies = [
            pltpu.make_async_copy(
                in_ref.at[pl.ds(group * each, each)], held.at[pl.ds(group * each, each)], sems.at[group]
            )
            for group in range(groups)
        ]
        for copy in copies:
            copy.start()
        for group in range(groups):
            copies[group].wait()
            for span in range(spans):
                at = slice(span * rows_local, (span + 1) * rows_local)
                total = held[group * each, span].astype(jnp.float32)
                for owner in range(group * each + 1, (group + 1) * each):
                    total = total + held[owner, span].astype(jnp.float32)
                if group:
                    total = sums[at] + total
                if group < groups - 1:
                    sums[at] = total
                else:
                    out_ref[at] = (
                        (1.0 - RESIDUAL_SHARE) * total + RESIDUAL_SHARE * init_ref[at]
                    ).astype(jnp.bfloat16)

    return pl.pallas_call(
        kernel,
        out_shape=jax.ShapeDtypeStruct((spans * rows_local, width), jnp.bfloat16),
        in_specs=[IN_HBM, IN_VMEM],
        out_specs=IN_VMEM,
        scratch_shapes=[
            pltpu.VMEM(arrived.shape, jnp.bfloat16),
            pltpu.SemaphoreType.DMA((groups,)),
            pltpu.VMEM((spans * rows_local, width), jnp.float32),
        ],
        compiler_params=vmem_params(16),
        cost_estimate=cost(arrived.size, 2 * arrived.size),
        name="collect",
    )(arrived, initial)


def replaced_columns(tiles, slots, select):
    spans, slot_count, side, _ = tiles.shape
    cols, picks = select.shape
    rows = slots.shape[1] // (cols // side) * side
    rows_local = picks // spans

    def kernel(slots_ref, tiles_ref, sel_ref, *refs):
        column_refs, (held, tile_sems, sends) = refs[:spans], refs[spans : spans + 3]
        kept = refs[spans + 3 :]
        copies = tile_copies(tiles_ref, held, tile_sems)
        for copy in copies:
            copy.start()
        outgoing = []
        for span in range(spans):
            used = (span + 1) * rows_local
            held[span, slot_count] = jnp.zeros((side, side), jnp.bfloat16)
            copies[span].wait()

            def put(at, part, span=span):
                kept[span][at] = part.astype(jnp.bfloat16)

            multiply(held, slots_ref, span, sel_ref, used, put)
            outgoing.append(pltpu.make_async_copy(kept[span], column_refs[span], sends.at[span]))
            outgoing[-1].start()
        for copy in outgoing:
            copy.wait()

    shapes = [(rows, (span + 1) * rows_local) for span in range(spans)]
    return pl.pallas_call(
        kernel,
        out_shape=tuple(jax.ShapeDtypeStruct(shape, jnp.bfloat16) for shape in shapes),
        in_specs=[IN_SMEM, IN_HBM, IN_VMEM],
        out_specs=(IN_HBM,) * spans,
        scratch_shapes=[
            *tile_scratch(tiles),
            pltpu.SemaphoreType.DMA((spans,)),
            *[pltpu.VMEM(shape, jnp.bfloat16) for shape in shapes],
        ],
        compiler_params=vmem_params(KERNEL_VMEM),
        cost_estimate=cost(2 * spans * rows * cols * picks, 2 * tiles.size + 6 * rows * picks),
        name="replaced_columns",
    )(slots, tiles, select)


def static_parts(tiles, slots, hist_slices, replaced):
    spans, slot_count, side, _ = tiles.shape
    layers, cols, width = hist_slices.shape
    rows = slots.shape[1] // (cols // side) * side
    kinds = layers - 2
    stored = kinds * width

    def kernel(slots_ref, tiles_ref, hist_ref, mask_ref, *refs):
        static_refs = refs[:kinds]
        held, tile_sems, hist, hist_sem, right, sums, sends = refs[kinds:]
        hist_copy = pltpu.make_async_copy(hist_ref.at[pl.ds(2, kinds)], hist, hist_sem)
        copies = tile_copies(tiles_ref, held, tile_sems)
        for copy in [hist_copy] + copies:
            copy.start()
        hist_copy.wait()
        outgoing = []
        for span in range(spans):
            held[span, slot_count] = jnp.zeros((side, side), jnp.bfloat16)
            for index in range(kinds):
                right[:, index * width : (index + 1) * width] = jnp.where(
                    mask_ref[span] > 0, jnp.zeros_like(hist[index]), hist[index]
                )
            copies[span].wait()

            def put(at, part, span=span):
                for index in range(kinds):
                    sums[index, span, at] = part[:, index * width : (index + 1) * width]

            multiply(held, slots_ref, span, right, stored, put)
            for index in range(kinds):
                outgoing.append(
                    pltpu.make_async_copy(
                        sums.at[index, span], static_refs[index].at[span], sends.at[index, span]
                    )
                )
                outgoing[-1].start()
        for copy in outgoing:
            copy.wait()

    return pl.pallas_call(
        kernel,
        out_shape=(jax.ShapeDtypeStruct((spans, rows, width), jnp.float32),) * kinds,
        in_specs=[IN_SMEM, IN_HBM, IN_HBM, IN_VMEM],
        out_specs=(IN_HBM,) * kinds,
        scratch_shapes=[
            *tile_scratch(tiles),
            pltpu.VMEM((kinds, cols, width), jnp.bfloat16),
            pltpu.SemaphoreType.DMA(()),
            pltpu.VMEM((cols, stored), jnp.bfloat16),
            pltpu.VMEM((kinds, spans, rows, width), jnp.float32),
            pltpu.SemaphoreType.DMA((kinds, spans)),
        ],
        compiler_params=vmem_params(KERNEL_VMEM),
        cost_estimate=cost(
            2 * spans * rows * cols * stored, 2 * tiles.size + spans * 4 * rows * stored
        ),
        name="static_parts",
    )(slots, tiles, hist_slices, replaced)


def fill_left(left, gath_ref, section, halves, parts, width):
    for half in range(halves):
        for part in range(parts):
            first = (half * parts + part) * width
            place = lax.rem(section - part + parts, parts)
            left[:, first : first + width] = gath_ref[half, place]


def layer_step(place, gathered, support, slices, static, columns, layer, beta, row_devices, resident):
    halves, parts, picks, width = gathered.shape
    spans, rows, _ = static.shape
    rows_local = rows // row_devices
    depth = halves * parts * width
    step = ROW_CHUNK // rows_local
    chunks = row_devices // step

    heavy = IN_VMEM if resident else IN_HBM
    small = (1, 16, 128)

    def kernel(place_ref, gath_ref, sup_ref, static_ref, *refs):
        slice_refs, column_refs = refs[:parts], refs[parts : parts + spans]
        out_ref, left, left_sems, sup, sup_sem, right, right_sem, stat, stat_sems, cols_sems, sums, out_sems = refs[parts + spans : -spans]
        cols = refs[-spans:]
        section = place_ref[0]
        apart = lax.rem(section - layer + parts, parts)
        incoming = []
        for half in range(halves):
            for part in range(parts):
                first = (half * parts + part) * width
                incoming.append(
                    pltpu.make_async_copy(
                        gath_ref.at[half, lax.rem(section - part + parts, parts)],
                        left.at[:, first : first + width],
                        left_sems.at[half, part],
                    )
                )
        incoming.append(pltpu.make_async_copy(sup_ref, sup, sup_sem))
        for copy in incoming:
            copy.start()
        for by in range(parts):
            @pl.when(apart == by)
            def _():
                pltpu.make_async_copy(slice_refs[by], right, right_sem).start()

        later = [()] * spans
        if resident:
            cols, stat = column_refs, static_ref
        else:
            for span in range(spans):
                later[span] = (
                    pltpu.make_async_copy(column_refs[span], cols[span], cols_sems.at[span]),
                    pltpu.make_async_copy(static_ref.at[span], stat.at[span], stat_sems.at[span]),
                )
                for copy in later[span]:
                    copy.start()

        for copy in incoming:
            copy.wait()
        pltpu.make_async_copy(slice_refs[0], right, right_sem).wait()
        projected = jnp.dot(left[...], right[...], preferred_element_type=jnp.float32)
        fresh = jnp.maximum(
            (1.0 - beta) * sup[...].astype(jnp.float32) + beta * projected, 0.0
        ).astype(jnp.bfloat16)
        outgoing = []
        for span in range(spans):
            used = (span + 1) * rows_local
            for copy in later[span]:
                copy.wait()
            for chunk in range(chunks):
                first = chunk * step
                at = slice(chunk * ROW_CHUNK, (chunk + 1) * ROW_CHUNK)
                part = stat[span, at] + jnp.dot(
                    cols[span][at], fresh[:used], preferred_element_type=jnp.float32
                )
                sums[span, first : first + step] = part.astype(jnp.bfloat16).reshape(
                    step, rows_local, width
                )
                outgoing.append(
                    pltpu.make_async_copy(
                        sums.at[span, first : first + step],
                        out_ref.at[first : first + step, span],
                        out_sems.at[span, chunk],
                    )
                )
                outgoing[-1].start()
        for copy in outgoing:
            copy.wait()

    return pl.pallas_call(
        kernel,
        out_shape=jax.ShapeDtypeStruct((row_devices, spans, rows_local, width), jnp.bfloat16),
        in_specs=[IN_SMEM, IN_HBM, IN_HBM, heavy] + [IN_HBM] * parts + [heavy] * spans,
        out_specs=IN_HBM,
        scratch_shapes=[
            pltpu.VMEM((picks, depth), jnp.bfloat16),
            pltpu.SemaphoreType.DMA((halves, parts)),
            pltpu.VMEM((picks, width), jnp.bfloat16),
            pltpu.SemaphoreType.DMA(()),
            pltpu.VMEM((depth, width), jnp.bfloat16),
            pltpu.SemaphoreType.DMA(()),
            pltpu.VMEM(small if resident else static.shape, jnp.float32),
            pltpu.SemaphoreType.DMA((spans,)),
            pltpu.SemaphoreType.DMA((spans,)),
            pltpu.VMEM((spans, row_devices, rows_local, width), jnp.bfloat16),
            pltpu.SemaphoreType.DMA((spans, chunks)),
            *[pltpu.VMEM(small if resident else each.shape, jnp.bfloat16) for each in columns],
        ],
        compiler_params=vmem_params(16 if resident else KERNEL_VMEM),
        cost_estimate=cost(
            2 * picks * depth * width + 2 * spans * rows * width * picks,
            6 * spans * rows * width + 2 * spans * rows * picks,
        ),
        name="layer_step",
    )(place, gathered, support, static, *slices, *columns)


def whole_rows(place, betas, gathered, weight_cols, earlier, layer):
    halves, parts, picks, width = gathered.shape
    depth, half = weight_cols.shape

    def kernel(place_ref, betas_ref, gath_ref, w_ref, *refs):
        earlier_ref, out_ref, left, own = refs
        section, feat = place_ref[0], place_ref[1]

        @pl.when(section == layer)
        def _():
            beta = betas_ref[layer]
            fill_left(left, gath_ref, section, halves, parts, width)
            for part in range(parts):
                own[:, part * width : (part + 1) * width] = gath_ref[
                    feat, lax.rem(section - part + parts, parts)
                ]
            projected = jnp.dot(left[...], w_ref[...], preferred_element_type=jnp.float32)
            out_ref[...] = jnp.maximum(
                (1.0 - beta) * own[...].astype(jnp.float32) + beta * projected, 0.0
            ).astype(jnp.bfloat16)

        @pl.when(section != layer)
        def _():
            out_ref[...] = earlier_ref[...]

    operands = [gathered, weight_cols, earlier]
    return pl.pallas_call(
        kernel,
        out_shape=jax.ShapeDtypeStruct((picks, half), jnp.bfloat16),
        in_specs=[pl.BlockSpec(memory_space=pltpu.SMEM)] * 2
        + [pl.BlockSpec(memory_space=pltpu.VMEM)] * len(operands),
        scratch_shapes=[
            pltpu.VMEM((picks, depth), jnp.bfloat16),
            pltpu.VMEM((picks, half), jnp.bfloat16),
        ],
        compiler_params=vmem_params(16),
        cost_estimate=cost(2 * picks * depth * half, 2 * (picks * depth + depth * half)),
        name="whole_rows",
    )(place, betas, *operands)


def replace_rows(stored, ids, fresh):
    owned, half = stored.shape
    picks = ids.shape[1]
    chunk = 512

    def kernel(stored_ref, ids_ref, fresh_ref, out_ref):
        first = pl.program_id(0) * chunk
        vertex = first + lax.broadcasted_iota(jnp.int32, (chunk, picks), 0)
        hits = (vertex == ids_ref[...]).astype(jnp.float32)
        placed = jnp.dot(
            hits.astype(jnp.bfloat16), fresh_ref[...], preferred_element_type=jnp.float32
        )
        found = jnp.sum(hits, axis=1, keepdims=True) > 0
        out_ref[...] = jnp.where(found, placed, stored_ref[...].astype(jnp.float32)).astype(
            jnp.bfloat16
        )

    return pl.pallas_call(
        kernel,
        out_shape=jax.ShapeDtypeStruct((owned, half), jnp.bfloat16),
        grid=(owned // chunk,),
        in_specs=[
            pl.BlockSpec((chunk, half), lambda i: (i, 0)),
            pl.BlockSpec((1, picks), lambda i: (0, 0)),
            pl.BlockSpec((picks, half), lambda i: (0, 0)),
        ],
        out_specs=pl.BlockSpec((chunk, half), lambda i: (i, 0)),
        compiler_params=vmem_params(KERNEL_VMEM),
        cost_estimate=cost(2 * owned * picks * half, 4 * owned * half),
        name="replace_rows",
    )(stored, ids, fresh)


def shards(features, history, weights, tile_values, tile_rows, tile_cols, tile_counts, span_ids):
    spans, rows_local = span_ids.shape
    side = tile_values.shape[2]
    owned, half = features.shape
    layers = lax.axis_size("section")
    row_devices = lax.axis_size("vertex")
    section = lax.axis_index("section")
    width = half // layers
    picks = spans * rows_local
    depth = weights.shape[1]
    betas = [math.log(BETA_SCALE / (layer + 1) + 1.0) for layer in range(layers)]
    place = jnp.stack([section, lax.axis_index("feat")]).astype(jnp.int32)
    beta_table = jnp.array(betas, jnp.float32)

    stored = history[0]
    hist_slices = lax.all_to_all(section_slices(stored, layers), "section", 0, 0, tiled=True)

    select, replaced = selection(span_ids, owned, width)
    ids = span_ids.reshape(1, picks)
    feat_slice = lax.dynamic_slice_in_dim(features, section * width, width, 1)
    initial_half = jnp.take(features, ids[0], axis=0)
    initial = lax.dynamic_slice_in_dim(initial_half, section * width, width, 1).astype(jnp.float32)
    col_blocks = owned // side
    blocks = rows_local * row_devices // side * col_blocks
    slot_count = tile_rows.shape[1]
    listed = jnp.arange(slot_count)[None, :]
    key = jnp.where(listed < tile_counts, tile_rows * col_blocks + tile_cols, blocks)
    here = key[:, :, None] == jnp.arange(blocks)[None, None, :]
    slots = slot_count + jnp.sum(
        jnp.where(here, listed[:, :, None] - slot_count, 0), axis=1, dtype=jnp.int32
    )
    columns = replaced_columns(tile_values, slots, select)
    hist_slices, replaced, feat_slice, initial, slots, columns = lax.optimization_barrier(
        (hist_slices, replaced, feat_slice, initial, slots, columns)
    )
    partial, static_one = first_partial(
        tile_values, slots, hist_slices, feat_slice, replaced, row_devices
    )
    own_weights = after(weights[0], partial)
    statics = [static_one, *static_parts(tile_values, slots, after(hist_slices, partial), replaced)]
    by_distance = [
        lax.dynamic_slice_in_dim(own_weights, (section + by) % layers * width, width, 1)
        for by in range(layers)
    ]
    weight_slices = [by_distance[0]] + [
        rotated(by_distance[by], "section", by) for by in range(1, layers)
    ]

    rows_kept, table = initial_half, None
    for layer in range(layers):
        if layer == layers - 1:
            before = rotated(rows_kept, "section", 1)
            table = replace_rows(stored, ids, before)
        arrived = lax.all_to_all(partial, "vertex", 0, 0, tiled=True)
        if layer == 0:
            arrived, statics, weight_slices = lax.optimization_barrier(
                (arrived, statics, weight_slices)
            )
        if table is not None:
            arrived, table = lax.optimization_barrier((arrived, table))
        support = collect(arrived, initial)
        near = jnp.stack([support] + [rotated(support, "section", by) for by in range(1, layers)])
        gathered = lax.all_gather(near, "feat", axis=0)
        if layer < layers - 1:
            partial = layer_step(
                place,
                gathered,
                support,
                weight_slices,
                statics[layer],
                columns,
                layer,
                betas[layer],
                row_devices,
                layer > 0,
            )
        rows_kept = whole_rows(place, beta_table, gathered, own_weights, rows_kept, layer)
    return (rows_kept.reshape(1, spans, rows_local, half), table[None])


def solution(mesh):
    placed = (
        P("vertex", "feat"),
        P("section", "vertex", "feat"),
        P("section", None, "feat"),
        P(None, "vertex", None, None),
        P(None, "vertex"),
        P(None, "vertex"),
        P(None, "vertex"),
        P(None, "vertex"),
    )
    return jax.shard_map(
        shards,
        mesh=mesh,
        in_specs=placed,
        out_specs=(P("section", None, "vertex", "feat"), P("section", "vertex", "feat")),
        check_vma=False,
    )
```

```python
import math

import jax
import jax.numpy as jnp
from jax import lax
from jax.experimental import pallas as pl
from jax.experimental.pallas import tpu as pltpu
from jax.sharding import PartitionSpec as P

RESIDUAL_SHARE = 0.2
BETA_SCALE = 0.5
MIB = 1 << 20
ROW_CHUNK = 1024
KERNEL_VMEM = 58
IN_HBM = pl.BlockSpec(memory_space=pltpu.HBM)
IN_VMEM = pl.BlockSpec(memory_space=pltpu.VMEM)
IN_SMEM = pl.BlockSpec(memory_space=pltpu.SMEM)


def rotated(array, axis, by):
    devices = lax.axis_size(axis)
    return lax.ppermute(array, axis, [(i, (i + by) % devices) for i in range(devices)])


def after(array, earlier):
    return lax.optimization_barrier((array, earlier))[0]


def vmem_params(mib):
    return pltpu.CompilerParams(vmem_limit_bytes=mib * MIB)


def cost(flops, bytes_accessed):
    return pl.CostEstimate(flops=flops, transcendentals=0, bytes_accessed=bytes_accessed)


def rows_from(tiles_ref, slots_ref, span, first, count, col_blocks):
    lines = []
    for row in range(count):
        base = (first + row) * col_blocks
        lines.append(
            jnp.concatenate(
                [tiles_ref[span, slots_ref[span, base + col]] for col in range(col_blocks)], axis=1
            )
        )
    return jnp.concatenate(lines, axis=0)


def multiply(tiles_ref, slots_ref, span, right, width, put, unrolled=False):
    side = tiles_ref.shape[-1]
    col_blocks = right.shape[0] // side
    row_blocks = slots_ref.shape[1] // col_blocks
    step = ROW_CHUNK // side

    def chunk(first):
        left = rows_from(tiles_ref, slots_ref, span, first, step, col_blocks)
        part = jnp.dot(left, right[:, :width], preferred_element_type=jnp.float32)
        put(pl.ds(pl.multiple_of(first * side, side), ROW_CHUNK), part)

    if unrolled:
        for first in range(0, row_blocks, step):
            chunk(first)
    else:
        pl.loop(0, row_blocks, step=step)(chunk)


def tile_copies(tiles_ref, held, sems):
    spans, slots = tiles_ref.shape[:2]
    return [
        pltpu.make_async_copy(
            tiles_ref.at[span], held.at[span, pl.ds(0, slots)], sems.at[span]
        )
        for span in range(spans)
    ]


def tile_scratch(tiles):
    spans, slots, side, _ = tiles.shape
    return [pltpu.VMEM((spans, slots + 1, side, side), jnp.bfloat16), pltpu.SemaphoreType.DMA((spans,))]


def first_partial(tiles, slots, hist_slices, feats, replaced, row_devices):
    spans, slot_count, side, _ = tiles.shape
    _, cols, width = hist_slices.shape
    col_blocks = cols // side
    row_blocks = slots.shape[1] // col_blocks

    def kernel(slots_ref, tiles_ref, hist_ref, feat_ref, mask_ref, out_ref, static_ref, held, tile_sems, hist, hist_sem, table, sums, out_sems, static, static_sems):
        hist_copy = pltpu.make_async_copy(hist_ref.at[pl.ds(0, 2)], hist, hist_sem)
        copies = tile_copies(tiles_ref, held, tile_sems)
        for copy in [hist_copy] + copies:
            copy.start()
        hist_copy.wait()
        outgoing = []
        for span in range(spans):
            held[span, slot_count] = jnp.zeros((side, side), jnp.bfloat16)
            replaces = mask_ref[span] > 0
            table[:, :width] = jnp.where(replaces, feat_ref[...], hist[0])
            table[:, width:] = jnp.where(replaces, jnp.zeros_like(hist[1]), hist[1])
            copies[span].wait()

            def put(at, part, span=span):
                sums[span, at] = part[:, :width].astype(jnp.bfloat16)
                static[span, at] = part[:, width:]

            multiply(held, slots_ref, span, table, 2 * width, put, unrolled=True)
            outgoing.append(
                pltpu.make_async_copy(static.at[span], static_ref.at[span], static_sems.at[span])
            )
            outgoing[-1].start()
            for device in range(row_devices):
                outgoing.append(
                    pltpu.make_async_copy(
                        sums.at[span, pl.ds(device * side, side)],
                        out_ref.at[device, span],
                        out_sems.at[span, device],
                    )
                )
                outgoing[-1].start()
        for copy in outgoing:
            copy.wait()

    return pl.pallas_call(
        kernel,
        out_shape=(
            jax.ShapeDtypeStruct((row_devices, spans, side, width), jnp.bfloat16),
            jax.ShapeDtypeStruct((spans, row_blocks * side, width), jnp.float32),
        ),
        in_specs=[IN_SMEM, IN_HBM, IN_HBM, IN_VMEM, IN_VMEM],
        out_specs=(IN_HBM, IN_HBM),
        scratch_shapes=[
            *tile_scratch(tiles),
            pltpu.VMEM((2, cols, width), jnp.bfloat16),
            pltpu.SemaphoreType.DMA(()),
            pltpu.VMEM((cols, 2 * width), jnp.bfloat16),
            pltpu.VMEM((spans, row_blocks * side, width), jnp.bfloat16),
            pltpu.SemaphoreType.DMA((spans, row_devices)),
            pltpu.VMEM((spans, row_blocks * side, width), jnp.float32),
            pltpu.SemaphoreType.DMA((spans,)),
        ],
        compiler_params=vmem_params(KERNEL_VMEM),
        cost_estimate=cost(4 * spans * row_blocks * side * cols * width, 2 * tiles.size),
        name="first_partial",
    )(slots, tiles, hist_slices, feats, replaced)


def section_slices(array, parts):
    rows, cols = array.shape
    width = cols // parts
    groups = 2
    each = rows // groups

    def kernel(in_ref, out_ref, held, in_sems, out_sems):
        moves = []
        for group in range(groups):
            at = pl.ds(group * each, each)
            for part in range(parts):
                moves.append(
                    (
                        pltpu.make_async_copy(
                            in_ref.at[at, pl.ds(part * width, width)],
                            held.at[part, at],
                            in_sems.at[part, group],
                        ),
                        pltpu.make_async_copy(
                            held.at[part, at], out_ref.at[part, at], out_sems.at[part, group]
                        ),
                    )
                )
        for first, _ in moves:
            first.start()
        for first, second in moves:
            first.wait()
            second.start()
        for _, second in moves:
            second.wait()

    return pl.pallas_call(
        kernel,
        out_shape=jax.ShapeDtypeStruct((parts, rows, width), array.dtype),
        in_specs=[IN_HBM],
        out_specs=IN_HBM,
        scratch_shapes=[
            pltpu.VMEM((parts, rows, width), array.dtype),
            pltpu.SemaphoreType.DMA((parts, groups)),
            pltpu.SemaphoreType.DMA((parts, groups)),
        ],
        compiler_params=vmem_params(KERNEL_VMEM),
        cost_estimate=cost(0, 4 * rows * cols),
        name="section_slices",
    )(array)


def selection(ids, owned, width):
    spans, rows_local = ids.shape
    picks = spans * rows_local
    chunk = 512

    def kernel(ids_ref, select_ref, mask_ref):
        first = pl.program_id(0) * chunk
        vertex = first + lax.broadcasted_iota(jnp.int32, (chunk, picks), 0)
        hits = (vertex == ids_ref[...]).astype(jnp.float32)
        select_ref[...] = hits.astype(jnp.bfloat16)
        total = jnp.zeros((chunk, 1), jnp.float32)
        for span in range(spans):
            part = hits[:, span * rows_local : (span + 1) * rows_local]
            total = total + jnp.sum(part, axis=1, keepdims=True)
            mask_ref[span] = jnp.broadcast_to(total, (chunk, width)).astype(jnp.bfloat16)

    return pl.pallas_call(
        kernel,
        out_shape=(
            jax.ShapeDtypeStruct((owned, picks), jnp.bfloat16),
            jax.ShapeDtypeStruct((spans, owned, width), jnp.bfloat16),
        ),
        grid=(owned // chunk,),
        in_specs=[pl.BlockSpec((1, picks), lambda i: (0, 0))],
        out_specs=(
            pl.BlockSpec((chunk, picks), lambda i: (i, 0)),
            pl.BlockSpec((spans, chunk, width), lambda i: (0, i, 0)),
        ),
        compiler_params=vmem_params(16),
        cost_estimate=cost(owned * picks, 4 * owned * picks),
        name="selection",
    )(ids.reshape(1, picks))


def collect(arrived, initial):
    owners, spans, rows_local, width = arrived.shape

    groups = 4
    each = owners // groups

    def kernel(in_ref, init_ref, out_ref, held, sems, sums):
        copies = [
            pltpu.make_async_copy(
                in_ref.at[pl.ds(group * each, each)], held.at[pl.ds(group * each, each)], sems.at[group]
            )
            for group in range(groups)
        ]
        for copy in copies:
            copy.start()
        for group in range(groups):
            copies[group].wait()
            for span in range(spans):
                at = slice(span * rows_local, (span + 1) * rows_local)
                total = held[group * each, span].astype(jnp.float32)
                for owner in range(group * each + 1, (group + 1) * each):
                    total = total + held[owner, span].astype(jnp.float32)
                if group:
                    total = sums[at] + total
                if group < groups - 1:
                    sums[at] = total
                else:
                    out_ref[at] = (
                        (1.0 - RESIDUAL_SHARE) * total + RESIDUAL_SHARE * init_ref[at]
                    ).astype(jnp.bfloat16)

    return pl.pallas_call(
        kernel,
        out_shape=jax.ShapeDtypeStruct((spans * rows_local, width), jnp.bfloat16),
        in_specs=[IN_HBM, IN_VMEM],
        out_specs=IN_VMEM,
        scratch_shapes=[
            pltpu.VMEM(arrived.shape, jnp.bfloat16),
            pltpu.SemaphoreType.DMA((groups,)),
            pltpu.VMEM((spans * rows_local, width), jnp.float32),
        ],
        compiler_params=vmem_params(16),
        cost_estimate=cost(arrived.size, 2 * arrived.size),
        name="collect",
    )(arrived, initial)


def replaced_columns(tiles, slots, select):
    spans, slot_count, side, _ = tiles.shape
    cols, picks = select.shape
    rows = slots.shape[1] // (cols // side) * side
    rows_local = picks // spans

    def kernel(slots_ref, tiles_ref, sel_ref, *refs):
        column_refs, (held, tile_sems, sends) = refs[:spans], refs[spans : spans + 3]
        kept = refs[spans + 3 :]
        copies = tile_copies(tiles_ref, held, tile_sems)
        for copy in copies:
            copy.start()
        outgoing = []
        for span in range(spans):
            used = (span + 1) * rows_local
            held[span, slot_count] = jnp.zeros((side, side), jnp.bfloat16)
            copies[span].wait()

            def put(at, part, span=span):
                kept[span][at] = part.astype(jnp.bfloat16)

            multiply(held, slots_ref, span, sel_ref, used, put)
            outgoing.append(pltpu.make_async_copy(kept[span], column_refs[span], sends.at[span]))
            outgoing[-1].start()
        for copy in outgoing:
            copy.wait()

    shapes = [(rows, (span + 1) * rows_local) for span in range(spans)]
    return pl.pallas_call(
        kernel,
        out_shape=tuple(jax.ShapeDtypeStruct(shape, jnp.bfloat16) for shape in shapes),
        in_specs=[IN_SMEM, IN_HBM, IN_VMEM],
        out_specs=(IN_HBM,) * spans,
        scratch_shapes=[
            *tile_scratch(tiles),
            pltpu.SemaphoreType.DMA((spans,)),
            *[pltpu.VMEM(shape, jnp.bfloat16) for shape in shapes],
        ],
        compiler_params=vmem_params(KERNEL_VMEM),
        cost_estimate=cost(2 * spans * rows * cols * picks, 2 * tiles.size + 6 * rows * picks),
        name="replaced_columns",
    )(slots, tiles, select)


def static_parts(tiles, slots, hist_slices, replaced):
    spans, slot_count, side, _ = tiles.shape
    layers, cols, width = hist_slices.shape
    rows = slots.shape[1] // (cols // side) * side
    kinds = layers - 2
    stored = kinds * width

    def kernel(slots_ref, tiles_ref, hist_ref, mask_ref, *refs):
        static_refs = refs[:kinds]
        held, tile_sems, hist, hist_sem, right, sums, sends = refs[kinds:]
        hist_copy = pltpu.make_async_copy(hist_ref.at[pl.ds(2, kinds)], hist, hist_sem)
        copies = tile_copies(tiles_ref, held, tile_sems)
        for copy in [hist_copy] + copies:
            copy.start()
        hist_copy.wait()
        outgoing = []
        for span in range(spans):
            held[span, slot_count] = jnp.zeros((side, side), jnp.bfloat16)
            for index in range(kinds):
                right[:, index * width : (index + 1) * width] = jnp.where(
                    mask_ref[span] > 0, jnp.zeros_like(hist[index]), hist[index]
                )
            copies[span].wait()

            def put(at, part, span=span):
                for index in range(kinds):
                    sums[index, span, at] = part[:, index * width : (index + 1) * width]

            multiply(held, slots_ref, span, right, stored, put)
            for index in range(kinds):
                outgoing.append(
                    pltpu.make_async_copy(
                        sums.at[index, span], static_refs[index].at[span], sends.at[index, span]
                    )
                )
                outgoing[-1].start()
        for copy in outgoing:
            copy.wait()

    return pl.pallas_call(
        kernel,
        out_shape=(jax.ShapeDtypeStruct((spans, rows, width), jnp.float32),) * kinds,
        in_specs=[IN_SMEM, IN_HBM, IN_HBM, IN_VMEM],
        out_specs=(IN_HBM,) * kinds,
        scratch_shapes=[
            *tile_scratch(tiles),
            pltpu.VMEM((kinds, cols, width), jnp.bfloat16),
            pltpu.SemaphoreType.DMA(()),
            pltpu.VMEM((cols, stored), jnp.bfloat16),
            pltpu.VMEM((kinds, spans, rows, width), jnp.float32),
            pltpu.SemaphoreType.DMA((kinds, spans)),
        ],
        compiler_params=vmem_params(KERNEL_VMEM),
        cost_estimate=cost(
            2 * spans * rows * cols * stored, 2 * tiles.size + spans * 4 * rows * stored
        ),
        name="static_parts",
    )(slots, tiles, hist_slices, replaced)


def fill_left(left, gath_ref, section, halves, parts, width):
    for half in range(halves):
        for part in range(parts):
            first = (half * parts + part) * width
            place = lax.rem(section - part + parts, parts)
            left[:, first : first + width] = gath_ref[half, place]


def layer_step(place, gathered, support, slices, static, columns, layer, beta, row_devices, resident):
    halves, parts, picks, width = gathered.shape
    spans, rows, _ = static.shape
    rows_local = rows // row_devices
    depth = halves * parts * width
    step = ROW_CHUNK // rows_local
    chunks = row_devices // step

    heavy = IN_VMEM if resident else IN_HBM
    small = (1, 16, 128)

    def kernel(place_ref, gath_ref, sup_ref, static_ref, *refs):
        slice_refs, column_refs = refs[:parts], refs[parts : parts + spans]
        out_ref, left, left_sems, sup, sup_sem, right, right_sem, stat, stat_sems, cols_sems, sums, out_sems = refs[parts + spans : -spans]
        cols = refs[-spans:]
        section = place_ref[0]
        apart = lax.rem(section - layer + parts, parts)
        incoming = []
        for half in range(halves):
            for part in range(parts):
                first = (half * parts + part) * width
                incoming.append(
                    pltpu.make_async_copy(
                        gath_ref.at[half, lax.rem(section - part + parts, parts)],
                        left.at[:, first : first + width],
                        left_sems.at[half, part],
                    )
                )
        incoming.append(pltpu.make_async_copy(sup_ref, sup, sup_sem))
        for copy in incoming:
            copy.start()
        for by in range(parts):
            @pl.when(apart == by)
            def _():
                pltpu.make_async_copy(slice_refs[by], right, right_sem).start()

        later = [()] * spans
        if resident:
            cols, stat = column_refs, static_ref
        else:
            for span in range(spans):
                later[span] = (
                    pltpu.make_async_copy(column_refs[span], cols[span], cols_sems.at[span]),
                    pltpu.make_async_copy(static_ref.at[span], stat.at[span], stat_sems.at[span]),
                )
                for copy in later[span]:
                    copy.start()

        for copy in incoming:
            copy.wait()
        pltpu.make_async_copy(slice_refs[0], right, right_sem).wait()
        projected = jnp.dot(left[...], right[...], preferred_element_type=jnp.float32)
        fresh = jnp.maximum(
            (1.0 - beta) * sup[...].astype(jnp.float32) + beta * projected, 0.0
        ).astype(jnp.bfloat16)
        outgoing = []
        for span in range(spans):
            used = (span + 1) * rows_local
            for copy in later[span]:
                copy.wait()
            for chunk in range(chunks):
                first = chunk * step
                at = slice(chunk * ROW_CHUNK, (chunk + 1) * ROW_CHUNK)
                part = stat[span, at] + jnp.dot(
                    cols[span][at], fresh[:used], preferred_element_type=jnp.float32
                )
                sums[span, first : first + step] = part.astype(jnp.bfloat16).reshape(
                    step, rows_local, width
                )
                outgoing.append(
                    pltpu.make_async_copy(
                        sums.at[span, first : first + step],
                        out_ref.at[first : first + step, span],
                        out_sems.at[span, chunk],
                    )
                )
                outgoing[-1].start()
        for copy in outgoing:
            copy.wait()

    return pl.pallas_call(
        kernel,
        out_shape=jax.ShapeDtypeStruct((row_devices, spans, rows_local, width), jnp.bfloat16),
        in_specs=[IN_SMEM, IN_HBM, IN_HBM, heavy] + [IN_HBM] * parts + [heavy] * spans,
        out_specs=IN_HBM,
        scratch_shapes=[
            pltpu.VMEM((picks, depth), jnp.bfloat16),
            pltpu.SemaphoreType.DMA((halves, parts)),
            pltpu.VMEM((picks, width), jnp.bfloat16),
            pltpu.SemaphoreType.DMA(()),
            pltpu.VMEM((depth, width), jnp.bfloat16),
            pltpu.SemaphoreType.DMA(()),
            pltpu.VMEM(small if resident else static.shape, jnp.float32),
            pltpu.SemaphoreType.DMA((spans,)),
            pltpu.SemaphoreType.DMA((spans,)),
            pltpu.VMEM((spans, row_devices, rows_local, width), jnp.bfloat16),
            pltpu.SemaphoreType.DMA((spans, chunks)),
            *[pltpu.VMEM(small if resident else each.shape, jnp.bfloat16) for each in columns],
        ],
        compiler_params=vmem_params(16 if resident else KERNEL_VMEM),
        cost_estimate=cost(
            2 * picks * depth * width + 2 * spans * rows * width * picks,
            6 * spans * rows * width + 2 * spans * rows * picks,
        ),
        name="layer_step",
    )(place, gathered, support, static, *slices, *columns)


def whole_rows(place, betas, gathered, weight_cols, earlier, layer):
    halves, parts, picks, width = gathered.shape
    depth, half = weight_cols.shape

    def kernel(place_ref, betas_ref, gath_ref, w_ref, *refs):
        earlier_ref, out_ref, left, own = refs
        section, feat = place_ref[0], place_ref[1]

        @pl.when(section == layer)
        def _():
            beta = betas_ref[layer]
            fill_left(left, gath_ref, section, halves, parts, width)
            for part in range(parts):
                own[:, part * width : (part + 1) * width] = gath_ref[
                    feat, lax.rem(section - part + parts, parts)
                ]
            projected = jnp.dot(left[...], w_ref[...], preferred_element_type=jnp.float32)
            out_ref[...] = jnp.maximum(
                (1.0 - beta) * own[...].astype(jnp.float32) + beta * projected, 0.0
            ).astype(jnp.bfloat16)

        @pl.when(section != layer)
        def _():
            out_ref[...] = earlier_ref[...]

    operands = [gathered, weight_cols, earlier]
    return pl.pallas_call(
        kernel,
        out_shape=jax.ShapeDtypeStruct((picks, half), jnp.bfloat16),
        in_specs=[pl.BlockSpec(memory_space=pltpu.SMEM)] * 2
        + [pl.BlockSpec(memory_space=pltpu.VMEM)] * len(operands),
        scratch_shapes=[
            pltpu.VMEM((picks, depth), jnp.bfloat16),
            pltpu.VMEM((picks, half), jnp.bfloat16),
        ],
        compiler_params=vmem_params(16),
        cost_estimate=cost(2 * picks * depth * half, 2 * (picks * depth + depth * half)),
        name="whole_rows",
    )(place, betas, *operands)


def replace_rows(stored, ids, fresh):
    owned, half = stored.shape
    picks = ids.shape[1]
    chunk = 512

    def kernel(stored_ref, ids_ref, fresh_ref, out_ref):
        first = pl.program_id(0) * chunk
        vertex = first + lax.broadcasted_iota(jnp.int32, (chunk, picks), 0)
        hits = (vertex == ids_ref[...]).astype(jnp.float32)
        placed = jnp.dot(
            hits.astype(jnp.bfloat16), fresh_ref[...], preferred_element_type=jnp.float32
        )
        found = jnp.sum(hits, axis=1, keepdims=True) > 0
        out_ref[...] = jnp.where(found, placed, stored_ref[...].astype(jnp.float32)).astype(
            jnp.bfloat16
        )

    return pl.pallas_call(
        kernel,
        out_shape=jax.ShapeDtypeStruct((owned, half), jnp.bfloat16),
        grid=(owned // chunk,),
        in_specs=[
            pl.BlockSpec((chunk, half), lambda i: (i, 0)),
            pl.BlockSpec((1, picks), lambda i: (0, 0)),
            pl.BlockSpec((picks, half), lambda i: (0, 0)),
        ],
        out_specs=pl.BlockSpec((chunk, half), lambda i: (i, 0)),
        compiler_params=vmem_params(KERNEL_VMEM),
        cost_estimate=cost(2 * owned * picks * half, 4 * owned * half),
        name="replace_rows",
    )(stored, ids, fresh)


def shards(features, history, weights, tile_values, tile_rows, tile_cols, tile_counts, span_ids):
    spans, rows_local = span_ids.shape
    side = tile_values.shape[2]
    owned, half = features.shape
    layers = lax.axis_size("section")
    row_devices = lax.axis_size("vertex")
    section = lax.axis_index("section")
    width = half // layers
    picks = spans * rows_local
    depth = weights.shape[1]
    betas = [math.log(BETA_SCALE / (layer + 1) + 1.0) for layer in range(layers)]
    place = jnp.stack([section, lax.axis_index("feat")]).astype(jnp.int32)
    beta_table = jnp.array(betas, jnp.float32)

    stored = history[0]
    hist_slices = lax.all_to_all(section_slices(stored, layers), "section", 0, 0, tiled=True)

    select, replaced = selection(span_ids, owned, width)
    ids = span_ids.reshape(1, picks)
    feat_slice = lax.dynamic_slice_in_dim(features, section * width, width, 1)
    initial_half = jnp.take(features, ids[0], axis=0)
    initial = lax.dynamic_slice_in_dim(initial_half, section * width, width, 1).astype(jnp.float32)
    col_blocks = owned // side
    blocks = rows_local * row_devices // side * col_blocks
    slot_count = tile_rows.shape[1]
    listed = jnp.arange(slot_count)[None, :]
    key = jnp.where(listed < tile_counts, tile_rows * col_blocks + tile_cols, blocks)
    here = key[:, :, None] == jnp.arange(blocks)[None, None, :]
    slots = slot_count + jnp.sum(
        jnp.where(here, listed[:, :, None] - slot_count, 0), axis=1, dtype=jnp.int32
    )
    columns = replaced_columns(tile_values, slots, select)
    hist_slices, replaced, feat_slice, initial, slots, columns = lax.optimization_barrier(
        (hist_slices, replaced, feat_slice, initial, slots, columns)
    )
    partial, static_one = first_partial(
        tile_values, slots, hist_slices, feat_slice, replaced, row_devices
    )
    own_weights = after(weights[0], partial)
    statics = [static_one, *static_parts(tile_values, slots, after(hist_slices, partial), replaced)]
    by_distance = [
        lax.dynamic_slice_in_dim(own_weights, (section + by) % layers * width, width, 1)
        for by in range(layers)
    ]
    weight_slices = [by_distance[0]] + [
        rotated(by_distance[by], "section", by) for by in range(1, layers)
    ]

    rows_kept, table = initial_half, None
    for layer in range(layers):
        if layer == layers - 1:
            before = rotated(rows_kept, "section", 1)
            table = replace_rows(stored, ids, before)
        arrived = lax.all_to_all(partial, "vertex", 0, 0, tiled=True)
        if layer == 0:
            arrived, statics, weight_slices = lax.optimization_barrier(
                (arrived, statics, weight_slices)
            )
        if table is not None:
            arrived, table = lax.optimization_barrier((arrived, table))
        support = collect(arrived, initial)
        near = jnp.stack([support] + [rotated(support, "section", by) for by in range(1, layers)])
        gathered = lax.all_gather(near, "feat", axis=0)
        if layer < layers - 1:
            partial = layer_step(
                place,
                gathered,
                support,
                weight_slices,
                statics[layer],
                columns,
                layer,
                betas[layer],
                row_devices,
                True,
            )
        rows_kept = whole_rows(place, beta_table, gathered, own_weights, rows_kept, layer)
    return (rows_kept.reshape(1, spans, rows_local, half), table[None])


def solution(mesh):
    placed = (
        P("vertex", "feat"),
        P("section", "vertex", "feat"),
        P("section", None, "feat"),
        P(None, "vertex", None, None),
        P(None, "vertex"),
        P(None, "vertex"),
        P(None, "vertex"),
        P(None, "vertex"),
    )
    return jax.shard_map(
        shards,
        mesh=mesh,
        in_specs=placed,
        out_specs=(P("section", None, "vertex", "feat"), P("section", "vertex", "feat")),
        check_vma=False,
    )
```
